128 devices in a mesh: dp: 16 (over x, y), expert: 8 (over z, core).
Axes of the slice: x: 4, y: 4, z: 4, core: 2. Of those that a mesh axis runs over, the one named last changes fastest.
Arguments:
- layer_input: bfloat16 [16384, 2560], P(('dp', 'expert')), may hold values from -6 to 6
- output_grad: bfloat16 [16384, 2560], P(('dp', 'expert')), may hold values from -6 to 6
- expert_ids: int32 [16384, 2], P(('dp', 'expert')), may hold values from 0 to 7, all different within a row; in each aligned block of 128 rows (0 to 127, 128 to 255, ...) at most 48 rows name the same one
- gate_probs: bfloat16 [16384, 2], P(('dp', 'expert')), may hold values from 0.099609375 to 0.59765625
- gate_weight: float32 [8, 2560, 1536], P('expert', 'dp'), may hold values from -0.125 to 0.125
- up_weight: float32 [8, 2560, 1536], P('expert', 'dp'), may hold values from -0.125 to 0.125
- down_weight: float32 [8, 1536, 2560], P('expert', 'dp'), may hold values from -0.15625 to 0.15625
- gate_moment: float32 [8, 2560, 1536], P('expert', 'dp'), may hold values from -12 to 12
- up_moment: float32 [8, 2560, 1536], P('expert', 'dp'), may hold values from -12 to 12
- down_moment: float32 [8, 1536, 2560], P('expert', 'dp'), may hold values from -12 to 12
- gate_second: float32 [8, 2560, 1536], P('expert', 'dp'), may hold values from 1 to 100
- up_second: float32 [8, 2560, 1536], P('expert', 'dp'), may hold values from 1 to 100
- down_second: float32 [8, 1536, 2560], P('expert', 'dp'), may hold values from 1 to 100
Outputs:
- input_grad: bfloat16 [16384, 2560], P(('dp', 'expert'))
- prob_grad: bfloat16 [16384, 2], P(('dp', 'expert'))
- new_gate_weight: float32 [8, 2560, 1536], P('expert', 'dp')
- new_up_weight: float32 [8, 2560, 1536], P('expert', 'dp')
- new_down_weight: float32 [8, 1536, 2560], P('expert', 'dp')
- new_gate_moment: float32 [8, 2560, 1536], P('expert', 'dp')
- new_up_moment: float32 [8, 2560, 1536], P('expert', 'dp')
- new_down_moment: float32 [8, 1536, 2560], P('expert', 'dp')
- new_gate_second: float32 [8, 2560, 1536], P('expert', 'dp')
- new_up_second: float32 [8, 2560, 1536], P('expert', 'dp')
- new_down_second: float32 [8, 1536, 2560], P('expert', 'dp')
The draws below stay inside these ranges and needn't reach their ends.
Inputs may be any that keep to these rules, and one draw needn't show every extreme that they name: `expert_ids`: each token names 2 different experts. Among the (token, pick) pairs of one device's 128 tokens, no expert is named more than 48 times, and in every draw some device's tokens name some expert exactly 48 times.
All inputs are finite; a program needn't handle non-finite values.
Results may differ from the reference program's by a relative error of at most 0.025.
Values may be sent and summed in bfloat16 or wider, within the bound.
No kernel may reach another device: no remote copies, remote signals or barrier semaphores. Data moves between devices by JAX's collectives and lax.ppermute only.
A program may use at most 256 MiB of HBM per device.

```python
import math
import jax
import jax.numpy as jnp
import numpy as np
from jax import lax

D = 2560
FF = 1536
EXP_DEV = 1
PICKS = 2
TOK_DEV = 128
EXPERTS = 8
CAP = 48
TOKENS = 16384
N_DP = 16
N_EXPERT = 8


def levels(own_key, shape, shards, low, top_value):
    def one(dim, shards_of):
        steps = jax.random.uniform(jax.random.fold_in(jax.random.fold_in(own_key, 6), dim), (shards_of,), jnp.float32, low / len(shards), top_value / len(shards))
        return jnp.repeat(jnp.exp(steps), shape[dim] // shards_of).reshape((-1,) + (1,) * (len(shape) - dim - 1))

    gain = one(*shards[0])
    for cut in shards[1:]:
        gain = gain * one(*cut)
    return gain


def shared_out(key, own, number, rows, number_of, top, most, lean):
    order = jax.random.permutation(key, number_of)
    heavy_load, usual = portions_of(number_of, rows * top, most, lean, True), portions_of(number_of, rows * top, most, lean, False)
    places = jnp.arange(number_of)

    def named(lengths, rotation):
        used = int((lengths > 0).sum())
        fixed = max(1, used // 4)
        shifted = fixed + (places - fixed + rotation * (used - fixed)) % max(1, number_of - fixed)
        return jnp.zeros((number_of,), jnp.int32).at[order[jnp.where(places < fixed, places, shifted)]].set(jnp.asarray(lengths, jnp.int32))

    lengths = jnp.where(number % 4 == 0, named(heavy_load, number // 4), named(usual, number - number // 4 - 1))
    mixed = jax.random.permutation(jax.random.fold_in(own, 3), number_of)
    giver, taker = mixed[0:number_of // 2 * 2:2], mixed[1:number_of // 2 * 2:2]
    room = jnp.minimum(lengths[giver] - 1, most - lengths[taker]) // 2
    room = jnp.where((giver == order[0]) | (taker == order[0]) | (lengths[taker] == 0), 0, jnp.maximum(room, 0))
    shifted = jax.random.randint(jax.random.fold_in(own, 4), (number_of // 2,), 0, 1 << 20) % (room + 1)
    lengths = lengths.at[giver].add(-shifted).at[taker].add(shifted)
    labels = jnp.searchsorted(jnp.cumsum(lengths), jnp.arange(rows * top), side="right").astype(jnp.int32)
    grid = labels.reshape(top, rows).T
    grid = grid[jax.random.permutation(jax.random.fold_in(own, 1), rows)]
    rotation = jax.random.randint(jax.random.fold_in(own, 2), (rows, 1), 0, top)
    return jnp.take_along_axis(grid, (jnp.arange(top)[None, :] + rotation) % top, axis=1)


def portions_of(count, total, most, skew, full):
    weights = [(1 << 20) // math.isqrt(standing ** skew) + 1 for standing in range(1, count + 1)]
    largest = most if full else min(most, max(-(-total // count), total * weights[0] // sum(weights)))
    least = 1 if total - largest >= count - 1 else 0
    holding, surplus = [largest] + [least] * (count - 1), total - largest - least * (count - 1)
    while surplus > 0:
        free = [i for i in range(1, count) if holding[i] < largest] or [i for i in range(1, count) if holding[i] < most]
        mass, budget = sum([weights[i] for i in free]), surplus
        for i in free:
            extra = min(most - holding[i], max(1, budget * weights[i] // mass), surplus)
            holding[i] = holding[i] + extra
            surplus = surplus - extra
    return np.array(holding)


def noise(own_key, extent, width, most, pieces=(), held_as=jnp.bfloat16):
    drawn = jax.random.normal(own_key, extent, jnp.float32) * width
    if len(pieces) > 0:
        drawn = levels(own_key, extent, pieces, -0.22, 0.18) * drawn
    return jnp.clip(drawn, min=-most, max=most).astype(held_as)


def setup_inputs(seed: int = 0) -> dict:
    seeds = jax.random.split(jax.random.key(seed), 14)
    layer_input = noise(seeds[0], (TOKENS, D), 1.0, 6.0, ((0, 128),))
    output_grad = noise(seeds[1], (TOKENS, D), 1.0, 6.0, ((0, 128),))
    expert_ids_keys = jax.random.split(jax.random.fold_in(seeds[2], 1), TOKENS // TOK_DEV)
    expert_ids_turns = jax.random.permutation(jax.random.fold_in(seeds[2], 3), TOKENS // TOK_DEV)
    expert_ids = jax.vmap(lambda own, number: shared_out(jax.random.fold_in(seeds[2], 2), own, number, TOK_DEV, EXPERTS, PICKS, CAP, 2))(expert_ids_keys, expert_ids_turns).reshape((TOKENS, PICKS))
    gate_probs = jnp.clip(0.099609375 + 0.49804688 * jax.random.uniform(seeds[3], (TOKENS, PICKS), jnp.float32) ** levels(seeds[3], (TOKENS, PICKS), ((0, 128),), -0.2, 0.2), 0.099609375, 0.59765625).astype(jnp.bfloat16)
    gate_weight = noise(seeds[4], (EXPERTS, D, FF), D ** -0.5, 0.125, ((0, 8), (1, 16)), jnp.float32)
    up_weight = noise(seeds[5], (EXPERTS, D, FF), D ** -0.5, 0.125, ((0, 8), (1, 16)), jnp.float32)
    down_weight = noise(seeds[6], (EXPERTS, FF, D), FF ** -0.5, 0.15625, ((0, 8), (1, 16)), jnp.float32)
    gate_moment = noise(seeds[7], (EXPERTS, D, FF), 2.0, 12.0, ((0, 8), (1, 16)), jnp.float32)
    up_moment = noise(seeds[8], (EXPERTS, D, FF), 2.0, 12.0, ((0, 8), (1, 16)), jnp.float32)
    down_moment = noise(seeds[9], (EXPERTS, FF, D), 2.0, 12.0, ((0, 8), (1, 16)), jnp.float32)
    gate_second = jnp.clip(jnp.exp(math.log(100.0) - 4.6051702 * jax.random.uniform(seeds[10], (EXPERTS, D, FF), jnp.float32) ** levels(seeds[10], (EXPERTS, D, FF), ((0, 8), (1, 16)), -0.2, 0.2)), 1.0, 100.0)
    up_second = jnp.clip(jnp.exp(math.log(100.0) - 4.6051702 * jax.random.uniform(seeds[11], (EXPERTS, D, FF), jnp.float32) ** levels(seeds[11], (EXPERTS, D, FF), ((0, 8), (1, 16)), -0.2, 0.2)), 1.0, 100.0)
    down_second = jnp.clip(jnp.exp(math.log(100.0) - 4.6051702 * jax.random.uniform(seeds[12], (EXPERTS, FF, D), jnp.float32) ** levels(seeds[12], (EXPERTS, FF, D), ((0, 8), (1, 16)), -0.2, 0.2)), 1.0, 100.0)
    return {"layer_input": layer_input, "output_grad": output_grad, "expert_ids": expert_ids, "gate_probs": gate_probs, "gate_weight": gate_weight, "up_weight": up_weight, "down_weight": down_weight, "gate_moment": gate_moment, "up_moment": up_moment, "down_moment": down_moment, "gate_second": gate_second, "up_second": up_second, "down_second": down_second}


beta_one = 0.9
beta_two = 0.95
learn_rate = 0.003
decay_rate = 0.1
epsilon = 1e-08
correct_one = 1.0 - 2.6561398887587e-05
correct_two = 1.0 - 0.005920529220333

def slot_tables(flat_ids, expert_count, exp_dev, groups, capacity):
    onehot = (flat_ids[:, None] == jnp.arange(expert_count, dtype=jnp.int32)[None, :]).astype(jnp.int32)
    before = jnp.cumsum(onehot, axis=0) - onehot
    ranked = lax.optimization_barrier(jnp.sum(before * onehot, axis=1)).astype(jnp.int32)
    device = flat_ids // exp_dev
    local = flat_ids % exp_dev
    return ((local * groups + device) * capacity + ranked).astype(jnp.int32)

def build_rows(dest_slot, inputs, grads, probs):
    slots = EXPERTS * CAP
    owner = jnp.zeros((slots,), jnp.int32).at[dest_slot].set(jnp.arange(TOK_DEV * PICKS, dtype=jnp.int32) // PICKS)
    filled = jnp.zeros((slots,), jnp.int32).at[dest_slot].set(1) > 0
    zero_val = jnp.zeros((), inputs.dtype)
    send_input = jnp.where(filled[:, None], inputs[owner], zero_val)
    send_grad = jnp.where(filled[:, None], grads[owner], zero_val)
    send_gate = jnp.zeros((slots,), probs.dtype).at[dest_slot].set(probs.reshape(-1))
    return (send_input, send_grad, send_gate)

def expert_backward(args):
    x_rows, dy_rows, gate_rows, w_gate_up, w_down = args
    pre = jnp.dot(x_rows, w_gate_up, preferred_element_type=jnp.float32)
    gate_pre = pre[:, :FF]
    up_pre = pre[:, FF:]
    sigmoid_gate = jax.nn.sigmoid(gate_pre)
    silu_gate = gate_pre * sigmoid_gate
    hidden = (silu_gate * up_pre).astype(jnp.bfloat16)
    expert_out = jnp.dot(hidden, w_down, preferred_element_type=jnp.float32)
    prob_rows = lax.optimization_barrier(jnp.sum(dy_rows.astype(jnp.float32) * expert_out, axis=1)).astype(jnp.bfloat16)
    out_scaled = (gate_rows.astype(jnp.float32)[:, None] * dy_rows.astype(jnp.float32)).astype(jnp.bfloat16)
    hidden_grad = jnp.dot(out_scaled, w_down.T, preferred_element_type=jnp.float32)
    dsilu = sigmoid_gate * (1.0 + gate_pre * (1.0 - sigmoid_gate))
    pre_grad = jnp.concatenate((hidden_grad * up_pre * dsilu, hidden_grad * silu_gate), axis=1).astype(jnp.bfloat16)
    input_rows = jnp.dot(pre_grad, w_gate_up.T, preferred_element_type=jnp.float32).astype(jnp.bfloat16)
    term_gate_up = jnp.dot(x_rows.T, pre_grad, preferred_element_type=jnp.float32)
    term_down = jnp.dot(hidden.T, out_scaled, preferred_element_type=jnp.float32)
    return (input_rows, prob_rows, term_gate_up, term_down)

def adamw(weight, moment, second, grad):
    moment_new = beta_one * moment + (1.0 - beta_one) * grad
    second_new = beta_two * second + (1.0 - beta_two) * grad * grad
    update = moment_new / correct_one / (jnp.sqrt(second_new / correct_two) + epsilon)
    return (weight - learn_rate * (update + decay_rate * weight), moment_new, second_new)

def rounded(value):
    return lax.optimization_barrier(value.astype(jnp.bfloat16)).astype(jnp.float32)

def reference(layer_input, output_grad, expert_ids, gate_probs, gate_weight, up_weight, down_weight, gate_moment, up_moment, down_moment, gate_second, up_second, down_second):
    devices = N_DP * N_EXPERT
    rows = N_EXPERT * CAP
    flat_ids = expert_ids.reshape(devices, TOK_DEV * PICKS)
    dest_slot = jax.vmap(lambda ids: slot_tables(ids, EXPERTS, EXP_DEV, N_EXPERT, CAP))(flat_ids)
    send_input, send_grad, send_gate = jax.vmap(build_rows)(dest_slot, layer_input.reshape(devices, TOK_DEV, D), output_grad.reshape(devices, TOK_DEV, D), gate_probs.reshape(devices, TOK_DEV, PICKS))

    def regroup(buffer):
        shaped = buffer.reshape((N_DP, N_EXPERT, EXP_DEV, N_EXPERT, CAP) + buffer.shape[2:])
        order = (0, 3, 2, 1, 4) + tuple(range(5, shaped.ndim))
        return jnp.transpose(shaped, order).reshape((N_DP, EXPERTS, rows) + buffer.shape[2:])
    x_all = regroup(send_input)
    dy_all = regroup(send_grad)
    gate_all = regroup(send_gate)
    w_gate_up = jnp.concatenate((gate_weight, up_weight), axis=2).astype(jnp.bfloat16)
    w_down = down_weight.astype(jnp.bfloat16)

    def per_group(carry, piece):
        acc_gate_up, acc_down = carry
        x_rows, dy_rows, gate_rows = piece
        input_rows, prob_rows, term_gate_up, term_down = lax.map(expert_backward, (x_rows, dy_rows, gate_rows, w_gate_up, w_down))
        return ((acc_gate_up + rounded(term_gate_up), acc_down + rounded(term_down)), (input_rows, prob_rows))
    init = (jnp.zeros((EXPERTS, D, 2 * FF), jnp.float32), jnp.zeros((EXPERTS, FF, D), jnp.float32))
    (grad_gate_up, grad_down), (input_rows, prob_rows) = lax.scan(per_group, init, (x_all, dy_all, gate_all))

    def ungroup(buffer):
        shaped = buffer.reshape((N_DP, N_EXPERT, EXP_DEV, N_EXPERT, CAP) + buffer.shape[3:])
        order = (0, 3, 2, 1, 4) + tuple(range(5, shaped.ndim))
        return jnp.transpose(shaped, order).reshape((devices, EXPERTS * CAP) + buffer.shape[3:])
    back_rows = jax.vmap(lambda table, dest: table[dest])(ungroup(input_rows), dest_slot)
    input_grad = lax.optimization_barrier(jnp.sum(back_rows.reshape(devices, TOK_DEV, PICKS, D).astype(jnp.float32), axis=2)).astype(jnp.bfloat16).reshape(TOKENS, D)
    back_probs = jax.vmap(lambda table, dest: table[dest])(ungroup(prob_rows), dest_slot)
    prob_grad = back_probs.reshape(TOKENS, PICKS)
    new_gate_weight, new_gate_moment, new_gate_second = adamw(gate_weight, gate_moment, gate_second, grad_gate_up[:, :, :FF])
    new_up_weight, new_up_moment, new_up_second = adamw(up_weight, up_moment, up_second, grad_gate_up[:, :, FF:])
    new_down_weight, new_down_moment, new_down_second = adamw(down_weight, down_moment, down_second, grad_down)
    return (input_grad, prob_grad, new_gate_weight, new_up_weight, new_down_weight, new_gate_moment, new_up_moment, new_down_moment, new_gate_second, new_up_second, new_down_second)
```

```python
import jax
import jax.numpy as jnp
from jax import lax
from jax.sharding import PartitionSpec as P

beta_one = 0.9
beta_two = 0.95
learn_rate = 0.003
decay_rate = 0.1
epsilon = 1e-08
correct_one = 1.0 - 2.6561398887587e-05
correct_two = 1.0 - 0.005920529220333


def slot_tables(flat_ids, expert_count, exp_dev, groups, capacity):
    onehot = (flat_ids[:, None] == jnp.arange(expert_count, dtype=jnp.int32)[None, :]).astype(
        jnp.int32
    )
    before = jnp.cumsum(onehot, axis=0) - onehot
    ranked = jnp.sum(before * onehot, axis=1)
    device = flat_ids // exp_dev
    local = flat_ids % exp_dev
    return (local * groups + device) * capacity + ranked


def adamw(weight, moment, second, grad):
    moment_new = beta_one * moment + (1.0 - beta_one) * grad
    second_new = beta_two * second + (1.0 - beta_two) * grad * grad
    update = moment_new / correct_one / (jnp.sqrt(second_new / correct_two) + epsilon)
    return (weight - learn_rate * (update + decay_rate * weight), moment_new, second_new)


def body(
    layer_input,
    output_grad,
    expert_ids,
    gate_probs,
    gate_weight,
    up_weight,
    down_weight,
    gate_moment,
    up_moment,
    down_moment,
    gate_second,
    up_second,
    down_second,
):
    exp_dev = gate_weight.shape[0]
    hidden_units = gate_weight.shape[2]
    width = layer_input.shape[1]
    groups = lax.axis_size("expert")
    tok_count, picks = expert_ids.shape
    capacity = 3 * tok_count * picks // (2 * exp_dev * groups)
    slots = exp_dev * groups * capacity
    row_count = groups * capacity
    dest_slot = slot_tables(expert_ids.reshape(-1), exp_dev * groups, exp_dev, groups, capacity)
    owner = (
        jnp.zeros((slots,), jnp.int32)
        .at[dest_slot]
        .set(jnp.arange(tok_count * picks, dtype=jnp.int32) // picks)
    )
    filled = jnp.zeros((slots,), jnp.int32).at[dest_slot].set(1) > 0
    zero_val = jnp.zeros((), jnp.bfloat16)
    send_input = jnp.where(filled[:, None], layer_input[owner], zero_val).reshape(
        exp_dev, groups, capacity, width
    )
    send_grad = jnp.where(filled[:, None], output_grad[owner], zero_val).reshape(
        exp_dev, groups, capacity, width
    )
    send_gate = (
        jnp.zeros((slots,), jnp.bfloat16)
        .at[dest_slot]
        .set(gate_probs.reshape(-1))
        .reshape(exp_dev, groups, capacity)
    )
    w_gate_up_shard = jnp.concatenate((gate_weight, up_weight), axis=2).astype(jnp.bfloat16)
    w_down_shard = down_weight.astype(jnp.bfloat16)
    w_gate_up, w_down = (
        lax.all_gather(w_gate_up_shard, "dp", axis=1, tiled=True),
        lax.all_gather(w_down_shard, "dp", axis=1, tiled=True),
    )
    recv_input, recv_grad, recv_gate = (
        lax.all_to_all(send_input, "expert", split_axis=1, concat_axis=1, tiled=True),
        lax.all_to_all(send_grad, "expert", split_axis=1, concat_axis=1, tiled=True),
        lax.all_to_all(send_gate, "expert", split_axis=1, concat_axis=1, tiled=True),
    )
    x_rows = recv_input.reshape(exp_dev, row_count, width)
    dy_rows = recv_grad.reshape(exp_dev, row_count, width)
    gate_rows = recv_gate.reshape(exp_dev, row_count)
    pre = jnp.einsum("erd,edf->erf", x_rows, w_gate_up, preferred_element_type=jnp.float32)
    gate_pre = pre[:, :, :hidden_units]
    up_pre = pre[:, :, hidden_units:]
    sigmoid_gate = jax.nn.sigmoid(gate_pre)
    silu_gate = gate_pre * sigmoid_gate
    hidden_full = silu_gate * up_pre
    hidden = hidden_full.astype(jnp.bfloat16)
    gate_col = gate_rows.astype(jnp.float32)[:, :, None]
    raw_grad = jnp.einsum("erd,efd->erf", dy_rows, w_down, preferred_element_type=jnp.float32)
    prob_rows = jnp.sum(hidden.astype(jnp.float32) * raw_grad, axis=2).astype(jnp.bfloat16)
    hidden_scaled = (gate_col * hidden_full).astype(jnp.bfloat16)
    hidden_grad = gate_col * raw_grad
    dsilu = sigmoid_gate * (1.0 + gate_pre * (1.0 - sigmoid_gate))
    pre_grad = jnp.concatenate(
        (hidden_grad * up_pre * dsilu, hidden_grad * silu_gate), axis=2
    ).astype(jnp.bfloat16)
    input_rows = jnp.einsum(
        "erf,edf->erd", pre_grad, w_gate_up, preferred_element_type=jnp.float32
    ).astype(jnp.bfloat16)
    second = jnp.einsum(
        "erc,erd->ecd", hidden_scaled, dy_rows, preferred_element_type=jnp.float32
    ).astype(jnp.bfloat16)
    first = jnp.einsum(
        "erc,erf->ecf", x_rows, pre_grad, preferred_element_type=jnp.float32
    ).astype(jnp.bfloat16)
    grad_down = lax.psum_scatter(second[0], "dp", scatter_dimension=0, tiled=True)[None].astype(
        jnp.float32
    )
    grad_gate_up = lax.psum_scatter(first[0], "dp", scatter_dimension=0, tiled=True)[None].astype(
        jnp.float32
    )
    back_input, back_prob = (
        lax.all_to_all(
            input_rows.reshape(exp_dev, groups, capacity, width),
            "expert",
            split_axis=1,
            concat_axis=1,
            tiled=True,
        ),
        lax.all_to_all(
            prob_rows.reshape(exp_dev, groups, capacity),
            "expert",
            split_axis=1,
            concat_axis=1,
            tiled=True,
        ),
    )
    picked_rows = back_input.reshape(slots, width)[dest_slot].reshape(tok_count, picks, width)
    input_grad = jnp.sum(picked_rows.astype(jnp.float32), axis=1).astype(jnp.bfloat16)
    prob_grad = back_prob.reshape(slots)[dest_slot].reshape(tok_count, picks)
    new_gate_weight, new_gate_moment, new_gate_second = adamw(
        gate_weight, gate_moment, gate_second, grad_gate_up[:, :, :hidden_units]
    )
    new_up_weight, new_up_moment, new_up_second = adamw(
        up_weight, up_moment, up_second, grad_gate_up[:, :, hidden_units:]
    )
    new_down_weight, new_down_moment, new_down_second = adamw(
        down_weight, down_moment, down_second, grad_down
    )
    return (
        input_grad,
        prob_grad,
        new_gate_weight,
        new_up_weight,
        new_down_weight,
        new_gate_moment,
        new_up_moment,
        new_down_moment,
        new_gate_second,
        new_up_second,
        new_down_second,
    )


def solution(mesh):
    return jax.shard_map(
        body,
        mesh=mesh,
        in_specs=(
            P(("dp", "expert"), None),
            P(("dp", "expert"), None),
            P(("dp", "expert"), None),
            P(("dp", "expert"), None),
            P("expert", "dp", None),
            P("expert", "dp", None),
            P("expert", "dp", None),
            P("expert", "dp", None),
            P("expert", "dp", None),
            P("expert", "dp", None),
            P("expert", "dp", None),
            P("expert", "dp", None),
            P("expert", "dp", None),
        ),
        out_specs=(
            P(("dp", "expert"), None),
            P(("dp", "expert"), None),
            P("expert", "dp", None),
            P("expert", "dp", None),
            P("expert", "dp", None),
            P("expert", "dp", None),
            P("expert", "dp", None),
            P("expert", "dp", None),
            P("expert", "dp", None),
            P("expert", "dp", None),
            P("expert", "dp", None),
        ),
        check_vma=False,
    )
```

```python
import jax
import jax.numpy as jnp
from jax import lax
from jax.experimental import pallas as pl
from jax.experimental.pallas import tpu as pltpu
from jax.sharding import Mesh
from jax.sharding import PartitionSpec as P

beta_one = 0.9
beta_two = 0.95
learn_rate = 0.003
decay_rate = 0.1
epsilon = 1e-08
correct_one = 1.0 - 2.6561398887587e-05
correct_two = 1.0 - 0.005920529220333

LANES = 128
GROUPS = 8
f32 = jnp.float32
bf16 = jnp.bfloat16

PLUS = [(i, (i + 1) % 4) for i in range(4)]
MINUS = [(i, (i - 1) % 4) for i in range(4)]
SWAP = [(0, 1), (1, 0)]
PAIR_A = [(2 * yl + c, 2 * c + yl) for yl in range(2) for c in range(2)]
PAIR_B = [(2 * yl + c, 2 * c + 1 - yl) for yl in range(2) for c in range(2)]


def _cycle():
    pairs = []
    for x1 in range(2):
        for x0 in range(2):
            for yh in range(2):
                for yl in range(2):
                    for c in range(2):
                        src = (((x1 * 2 + x0) * 2 + yh) * 2 + yl) * 2 + c
                        dst = (((x1 * 2 + yh) * 2 + yl) * 2 + c) * 2 + x0
                        pairs.append((src, dst))
    return pairs


CYCLE = _cycle()
CYCLE_AXES = ("x", "yh", "yl", "c")


def back(pairs):
    return [(d, s) for s, d in pairs]


def piece_pairs(piece):
    db, dz = piece // 4, piece % 4
    return [
        (yl * 4 + z, (yl ^ db) * 4 + (z + dz) % 4) for yl in range(2) for z in range(4)
    ]


def adamw(weight, moment, second, grad):
    moment_new = beta_one * moment + (1.0 - beta_one) * grad
    second_new = beta_two * second + (1.0 - beta_two) * grad * grad
    update = moment_new / correct_one / (jnp.sqrt(second_new / correct_two) + epsilon)
    return (weight - learn_rate * (update + decay_rate * weight), moment_new, second_new)


def one_hots(place_ref, ids, capacity):
    tok = ids.shape[1]
    experts = lax.broadcasted_iota(jnp.int32, (GROUPS, tok), 0)
    named = [(experts == ids[k : k + 1, :]).astype(f32) for k in range(2)]
    earlier = (
        lax.broadcasted_iota(jnp.int32, (tok, tok), 0)
        < lax.broadcasted_iota(jnp.int32, (tok, tok), 1)
    ).astype(f32)
    count = jnp.dot(
        (named[0] + named[1]).astype(bf16), earlier.astype(bf16), preferred_element_type=f32
    )
    slot = lax.broadcasted_iota(jnp.int32, (GROUPS * capacity, tok), 0)
    hots = []
    for k in range(2):
        rank = jnp.sum(named[k] * count, axis=0, keepdims=True).astype(jnp.int32)
        expert = ids[k : k + 1, :]
        db = (expert + place_ref[0]) & 1
        dz = ((expert >> 1) + 4 - place_ref[1]) & 3
        dest = (db * 4 + dz) * capacity + rank
        hots.append((slot == dest).astype(f32))
    return hots


def pack_kernel(capacity, width, place_ref, ids_ref, probs_ref, x_ref, y_ref, *out_refs):
    first, second = one_hots(place_ref, ids_ref[...], capacity)
    hot = (first + second).astype(bf16)
    probs = probs_ref[...]
    gates = (first * probs[0:1, :] + second * probs[1:2, :]).astype(bf16)
    ones = jnp.ones((gates.shape[1], LANES), bf16)
    x_rows = jnp.dot(hot, x_ref[...], preferred_element_type=f32).astype(bf16)
    for k in range(GROUPS):
        out_refs[k][:, :width] = x_rows[k * capacity : (k + 1) * capacity]
    y_rows = jnp.dot(hot, y_ref[...], preferred_element_type=f32).astype(bf16)
    for k in range(GROUPS):
        out_refs[k][:, width : 2 * width] = y_rows[k * capacity : (k + 1) * capacity]
    g_rows = jnp.dot(gates, ones, preferred_element_type=f32).astype(bf16)
    for k in range(GROUPS):
        out_refs[k][:, 2 * width :] = g_rows[k * capacity : (k + 1) * capacity]


def unpack_kernel(capacity, width, place_ref, ids_ref, *refs):
    in_refs, x_ref, prob_ref, rows_ref = refs[:GROUPS], refs[-3], refs[-2], refs[-1]
    for k in range(GROUPS):
        rows_ref[k * capacity : (k + 1) * capacity, :] = in_refs[k][...]
    first, second = one_hots(place_ref, ids_ref[...], capacity)
    hot = (first + second).astype(bf16)
    x_ref[...] = lax.dot_general(
        hot, rows_ref[:, :width], (((0,), (0,)), ((), ())), preferred_element_type=f32
    ).astype(bf16)
    q_col = rows_ref[:, width:].astype(f32)
    prob_ref[0:1, :] = jnp.sum(first * q_col, axis=0, keepdims=True).astype(bf16)
    prob_ref[1:2, :] = jnp.sum(second * q_col, axis=0, keepdims=True).astype(bf16)


def vmem_specs(count):
    return [pl.BlockSpec(memory_space=pltpu.VMEM) for _ in range(count)]


def pack_rows(place, ids, probs, x, y, capacity):
    width = x.shape[1]
    piece = jax.ShapeDtypeStruct((capacity, 2 * width + LANES), bf16)
    return pl.pallas_call(
        lambda *refs: pack_kernel(capacity, width, *refs),
        out_shape=(piece,) * GROUPS,
        in_specs=[pl.BlockSpec(memory_space=pltpu.SMEM)] + vmem_specs(4),
        out_specs=tuple(vmem_specs(GROUPS)),
        compiler_params=pltpu.CompilerParams(vmem_limit_bytes=40 << 20),
        name="pack_rows",
    )(place, ids, probs, x, y)


def unpack_rows(place, ids, pieces, width, capacity):
    tok = ids.shape[1]
    return pl.pallas_call(
        lambda *refs: unpack_kernel(capacity, width, *refs),
        out_shape=(
            jax.ShapeDtypeStruct((tok, width), bf16),
            jax.ShapeDtypeStruct((2, tok), bf16),
        ),
        in_specs=[pl.BlockSpec(memory_space=pltpu.SMEM)] + vmem_specs(1 + GROUPS),
        out_specs=tuple(vmem_specs(2)),
        scratch_shapes=[pltpu.VMEM((GROUPS * capacity, width + LANES), bf16)],
        compiler_params=pltpu.CompilerParams(vmem_limit_bytes=40 << 20),
        name="unpack_rows",
    )(place, ids, *pieces)


def put(whole, part, row):
    return lax.dynamic_update_slice(whole, part, (row, 0))


def ring(part, half):
    left = lax.ppermute(part, "x", PLUS)
    right = lax.ppermute(part, "x", MINUS)
    far_top = lax.ppermute(left[:half], "x", PLUS)
    far_low = lax.ppermute(right[half:], "x", MINUS)
    return left, right, far_top, far_low


def gather_gate_up(part, x, yh):
    size = part.shape[0]
    other = lax.ppermute(part, "yh", SWAP)
    whole = jnp.zeros((8 * size, part.shape[1]), part.dtype)
    for piece, side in ((part, yh), (other, 1 - yh)):
        left, right, far_top, far_low = ring(piece, size // 2)

        def row(k):
            return size * (2 * ((x + k) % 4) + side)

        whole = put(whole, piece, row(0))
        whole = put(whole, left, row(3))
        whole = put(whole, right, row(1))
        whole = put(whole, far_top, row(2))
        whole = put(whole, far_low, row(2) + size // 2)
    return whole


def gather_down(part, x, yh):
    size = part.shape[0]
    other = lax.ppermute(part, "yh", SWAP)
    both = jnp.where(
        yh == 0, jnp.concatenate((part, other)), jnp.concatenate((other, part))
    )
    left, right, far_top, far_low = ring(both, size)
    whole = jnp.zeros((8 * size, part.shape[1]), part.dtype)
    for k, piece in ((0, both), (3, left), (1, right)):
        whole = put(whole, piece, 2 * size * ((x + k) % 4))
    whole = put(whole, far_top, 2 * size * ((x + 2) % 4))
    return put(whole, far_low, 2 * size * ((x + 2) % 4) + size)


def scatter_sum(terms, x, yh):
    size, n = terms.shape[0] // 8, terms.shape[1]

    def rows(k, side, count):
        return lax.dynamic_slice(
            terms, (size * (2 * ((x + k) % 4) + side), 0), (count * size, n)
        )

    def plus(*values):
        return sum(v.astype(f32) for v in values).astype(bf16)

    from_left = lax.ppermute(rows(2, 0, 1), "x", PLUS)
    from_right = lax.ppermute(rows(2, 1, 1), "x", MINUS)
    to_right = jnp.concatenate((plus(rows(1, 0, 1), from_left), rows(1, 1, 1)))
    to_left = jnp.concatenate((rows(3, 0, 1), plus(rows(3, 1, 1), from_right)))
    from_left = lax.ppermute(to_right, "x", PLUS)
    from_right = lax.ppermute(to_left, "x", MINUS)

    def mine(side):
        cut = lambda v: lax.dynamic_slice(v, (size * side, 0), (size, n))
        return plus(rows(0, side, 1), cut(from_left), cut(from_right))

    sent = lax.ppermute(mine(1 - yh), "yh", SWAP)
    return plus(mine(yh), sent)


def body(
    layer_input,
    output_grad,
    expert_ids,
    gate_probs,
    gate_weight,
    up_weight,
    down_weight,
    gate_moment,
    up_moment,
    down_moment,
    gate_second,
    up_second,
    down_second,
):
    x, yh, yl = lax.axis_index("x"), lax.axis_index("yh"), lax.axis_index("yl")
    z, c = lax.axis_index("z"), lax.axis_index("c")
    tok, picks = expert_ids.shape
    capacity = 3 * tok * picks // (2 * GROUPS)
    width = layer_input.shape[1]
    hidden_units = gate_weight.shape[2]
    quarter = hidden_units // 4
    half = hidden_units // 2
    rows = GROUPS * capacity

    gate_low, up_low = gate_weight[0].astype(bf16), up_weight[0].astype(bf16)

    def chunk(core):
        cuts = [
            w[:, (core + 2 * k) * quarter : (core + 2 * k + 1) * quarter]
            for w in (gate_low, up_low)
            for k in range(2)
        ]
        return jnp.concatenate(cuts, axis=1)

    chunks = (chunk(0), chunk(1))
    part_a = lax.ppermute(jnp.where(yl == 0, chunks[0], chunks[1]), ("yl", "c"), PAIR_A)
    part_b = lax.ppermute(jnp.where(yl == 0, chunks[1], chunks[0]), ("yl", "c"), PAIR_B)
    part = jnp.where(
        c == 0, jnp.concatenate((part_a, part_b)), jnp.concatenate((part_b, part_a))
    )
    down_part = lax.ppermute(down_weight[0].astype(bf16), CYCLE_AXES, CYCLE)
    w_gate_up = gather_gate_up(part, x, yh)
    w_down = gather_down(down_part, x, yh)

    place = jnp.stack((yl, z)).astype(jnp.int32)
    ids = expert_ids.T
    sent = pack_rows(place, ids, gate_probs.T.astype(f32), layer_input, output_grad, capacity)
    got = [sent[0]] + [
        lax.ppermute(sent[k], ("yl", "z"), piece_pairs(k)) for k in range(1, GROUPS)
    ]
    own = jnp.concatenate(got)
    other = lax.ppermute(own, "c", SWAP)
    x_rows = jnp.concatenate((own[:, :width], other[:, :width]))
    y_rows = jnp.concatenate((own[:, width : 2 * width], other[:, width : 2 * width]))
    gates = jnp.concatenate((own[:, 2 * width :], other[:, 2 * width :]))[:, :1].astype(f32)

    pre = jnp.dot(x_rows, w_gate_up, preferred_element_type=f32)
    gate_pre, up_pre = pre[:, :half], pre[:, half:]
    sigmoid_gate = jax.nn.sigmoid(gate_pre)
    silu_gate = gate_pre * sigmoid_gate
    hidden_full = silu_gate * up_pre
    hidden = hidden_full.astype(bf16)
    hidden_scaled = (gates * hidden_full).astype(bf16)
    down_term = lax.dot_general(
        hidden_scaled, y_rows, (((0,), (0,)), ((), ())), preferred_element_type=f32
    ).astype(bf16)
    grad_down = scatter_sum(down_term, x, yh)
    raw_grad = lax.dot_general(
        y_rows, w_down, (((1,), (1,)), ((), ())), preferred_element_type=f32
    )
    prob_rows = jnp.sum(hidden.astype(f32) * raw_grad, axis=1, keepdims=True)
    hidden_grad = gates * raw_grad
    dsilu = sigmoid_gate * (1.0 + gate_pre * (1.0 - sigmoid_gate))
    pre_grad = jnp.concatenate(
        (hidden_grad * up_pre * dsilu, hidden_grad * silu_gate), axis=1
    ).astype(bf16)
    gate_up_term = lax.dot_general(
        x_rows, pre_grad, (((0,), (0,)), ((), ())), preferred_element_type=f32
    ).astype(bf16)
    grad_gate_up = scatter_sum(gate_up_term, x, yh)

    def input_part(d_rows):
        return lax.dot_general(
            d_rows, w_gate_up, (((1,), (1,)), ((), ())), preferred_element_type=f32
        )

    far_rows = lax.ppermute(input_part(pre_grad[rows:]).astype(bf16), "c", SWAP)
    far_prob = lax.ppermute(
        jnp.broadcast_to(prob_rows[rows:], (rows, LANES)), "c", SWAP
    )
    near_rows = (input_part(pre_grad[:rows]) + far_rows.astype(f32)).astype(bf16)
    near_prob = (prob_rows[:rows] + far_prob).astype(bf16)
    packed = jnp.concatenate((near_rows, near_prob), axis=1)
    pieces = [packed[k * capacity : (k + 1) * capacity] for k in range(GROUPS)]
    returned = [pieces[0]] + [
        lax.ppermute(pieces[k], ("yl", "z"), back(piece_pairs(k))) for k in range(1, GROUPS)
    ]
    input_grad, prob_grad = unpack_rows(place, ids, returned, width, capacity)

    depth = gate_weight.shape[1]
    home_a = lax.ppermute(
        lax.dynamic_slice(grad_gate_up, (depth * c, 0), (depth, hidden_units)),
        ("yl", "c"),
        back(PAIR_A),
    ).astype(f32)
    home_b = lax.ppermute(
        lax.dynamic_slice(grad_gate_up, (depth * (1 - c), 0), (depth, hidden_units)),
        ("yl", "c"),
        back(PAIR_B),
    ).astype(f32)
    grad_down = lax.ppermute(grad_down, CYCLE_AXES, back(CYCLE)).astype(f32)
    even = jnp.where(yl == 0, home_a, home_b)
    odd = jnp.where(yl == 0, home_b, home_a)

    def natural(start):
        return jnp.concatenate(
            [
                v[:, start + k * quarter : start + (k + 1) * quarter]
                for k in range(2)
                for v in (even, odd)
            ],
            axis=1,
        )[None]

    new_gate_weight, new_gate_moment, new_gate_second = adamw(
        gate_weight, gate_moment, gate_second, natural(0)
    )
    new_up_weight, new_up_moment, new_up_second = adamw(
        up_weight, up_moment, up_second, natural(half)
    )
    new_down_weight, new_down_moment, new_down_second = adamw(
        down_weight, down_moment, down_second, grad_down[None]
    )
    return (
        input_grad,
        prob_grad.T,
        new_gate_weight,
        new_up_weight,
        new_down_weight,
        new_gate_moment,
        new_up_moment,
        new_down_moment,
        new_gate_second,
        new_up_second,
        new_down_second,
    )


def solution(mesh):
    fine = Mesh(mesh.devices.reshape(4, 2, 2, 4, 2), ("x", "yh", "yl", "z", "c"))
    tokens = P(("x", "yh", "yl", "z", "c"), None)
    weights = P(("z", "c"), ("x", "yh", "yl"), None)
    return jax.shard_map(
        body,
        mesh=fine,
        in_specs=(tokens,) * 4 + (weights,) * 9,
        out_specs=(tokens,) * 2 + (weights,) * 9,
        check_vma=False,
    )
```

```python
import jax
import jax.numpy as jnp
from jax import lax
from jax.experimental import pallas as pl
from jax.experimental.pallas import tpu as pltpu
from jax.sharding import Mesh
from jax.sharding import PartitionSpec as P

beta_one = 0.9
beta_two = 0.95
learn_rate = 0.003
decay_rate = 0.1
epsilon = 1e-08
correct_one = 1.0 - 2.6561398887587e-05
correct_two = 1.0 - 0.005920529220333

LANES = 128
GROUPS = 8
f32 = jnp.float32
bf16 = jnp.bfloat16

PLUS = [(i, (i + 1) % 4) for i in range(4)]
MINUS = [(i, (i - 1) % 4) for i in range(4)]
SWAP = [(0, 1), (1, 0)]
PAIR_A = [(2 * yl + c, 2 * c + yl) for yl in range(2) for c in range(2)]
PAIR_B = [(2 * yl + c, 2 * c + 1 - yl) for yl in range(2) for c in range(2)]


def _cycle():
    pairs = []
    for x1 in range(2):
        for x0 in range(2):
            for yh in range(2):
                for yl in range(2):
                    for c in range(2):
                        src = (((x1 * 2 + x0) * 2 + yh) * 2 + yl) * 2 + c
                        dst = (((x1 * 2 + yh) * 2 + yl) * 2 + c) * 2 + x0
                        pairs.append((src, dst))
    return pairs


CYCLE = _cycle()
CYCLE_AXES = ("x", "yh", "yl", "c")


def back(pairs):
    return [(d, s) for s, d in pairs]


def after(value, *earlier):
    return lax.optimization_barrier((value, earlier))[0]


def adamw(weight, moment, second, grad):
    moment_new = beta_one * moment + (1.0 - beta_one) * grad
    second_new = beta_two * second + (1.0 - beta_two) * grad * grad
    update = moment_new / correct_one / (jnp.sqrt(second_new / correct_two) + epsilon)
    return (weight - learn_rate * (update + decay_rate * weight), moment_new, second_new)


def one_hots(ids, capacity):
    tok = ids.shape[1]
    experts = lax.broadcasted_iota(jnp.int32, (GROUPS, tok), 0)
    named = [(experts == ids[k : k + 1, :]).astype(f32) for k in range(2)]
    earlier = (
        lax.broadcasted_iota(jnp.int32, (tok, tok), 0)
        < lax.broadcasted_iota(jnp.int32, (tok, tok), 1)
    ).astype(f32)
    count = jnp.dot(
        (named[0] + named[1]).astype(bf16), earlier.astype(bf16), preferred_element_type=f32
    )
    slot = lax.broadcasted_iota(jnp.int32, (GROUPS * capacity, tok), 0)
    hots = []
    for k in range(2):
        rank = jnp.sum(named[k] * count, axis=0, keepdims=True).astype(jnp.int32)
        expert = ids[k : k + 1, :]
        dest = ((expert & 1) * 4 + (expert >> 1)) * capacity + rank
        hots.append((slot == dest).astype(f32))
    return hots


def block_of(width):
    return 512 if width % 512 == 0 else width


def pack_kernel(capacity, width, ids_ref, probs_ref, x_ref, y_ref, out_ref):
    first, second = one_hots(ids_ref[...], capacity)
    hot = (first + second).astype(bf16)
    probs = probs_ref[...]
    gates = (first * probs[0:1, :] + second * probs[1:2, :]).astype(bf16)
    ones = jnp.ones((gates.shape[1], LANES), bf16)
    out_ref[:, 2 * width :] = jnp.dot(gates, ones, preferred_element_type=f32).astype(bf16)
    block = block_of(width)

    def step(i, carry):
        at = pl.multiple_of(i * block, block)
        cols = pl.ds(at, block)
        out_ref[:, cols] = jnp.dot(
            hot, x_ref[:, cols], preferred_element_type=f32
        ).astype(bf16)
        out_ref[:, pl.ds(pl.multiple_of(at + width, block), block)] = jnp.dot(
            hot, y_ref[:, cols], preferred_element_type=f32
        ).astype(bf16)
        return carry

    lax.fori_loop(0, width // block, step, 0)


def unpack_kernel(capacity, width, ids_ref, rows_ref, x_ref, prob_ref):
    first, second = one_hots(ids_ref[...], capacity)
    hot = (first + second).astype(bf16)
    block = block_of(width)

    def step(i, carry):
        cols = pl.ds(pl.multiple_of(i * block, block), block)
        x_ref[:, cols] = lax.dot_general(
            hot, rows_ref[:, cols], (((0,), (0,)), ((), ())), preferred_element_type=f32
        ).astype(bf16)
        return carry

    lax.fori_loop(0, width // block, step, 0)
    q_col = rows_ref[:, width:].astype(f32)
    prob_ref[0:1, :] = jnp.sum(first * q_col, axis=0, keepdims=True).astype(bf16)
    prob_ref[1:2, :] = jnp.sum(second * q_col, axis=0, keepdims=True).astype(bf16)


def vmem_specs(count):
    return [pl.BlockSpec(memory_space=pltpu.VMEM) for _ in range(count)]


def pack_rows(ids, probs, x, y, capacity):
    width = x.shape[1]
    return pl.pallas_call(
        lambda *refs: pack_kernel(capacity, width, *refs),
        out_shape=jax.ShapeDtypeStruct((GROUPS * capacity, 2 * width + LANES), bf16),
        in_specs=vmem_specs(4),
        out_specs=vmem_specs(1)[0],
        compiler_params=pltpu.CompilerParams(vmem_limit_bytes=40 << 20),
        name="pack_rows",
    )(ids, probs, x, y)


def unpack_rows(ids, rows, width, capacity):
    tok = ids.shape[1]
    return pl.pallas_call(
        lambda *refs: unpack_kernel(capacity, width, *refs),
        out_shape=(
            jax.ShapeDtypeStruct((tok, width), bf16),
            jax.ShapeDtypeStruct((2, tok), bf16),
        ),
        in_specs=vmem_specs(2),
        out_specs=tuple(vmem_specs(2)),
        compiler_params=pltpu.CompilerParams(vmem_limit_bytes=40 << 20),
        name="unpack_rows",
    )(ids, rows)


def put(whole, part, row):
    return lax.dynamic_update_slice(whole, part, (row, 0))


def neighbours(part):
    return lax.ppermute(part, "x", PLUS), lax.ppermute(part, "x", MINUS)


def far(left, right, half):
    return lax.ppermute(left[:half], "x", PLUS), lax.ppermute(right[half:], "x", MINUS)


def place_all(size, rows_of, sets):
    whole = jnp.zeros((8 * size, sets[0][0].shape[1]), bf16)
    for index, (part, left, right, top, low) in enumerate(sets):
        whole = put(whole, part, rows_of(0, index))
        whole = put(whole, left, rows_of(3, index))
        whole = put(whole, right, rows_of(1, index))
        whole = put(whole, top, rows_of(2, index))
        whole = put(whole, low, rows_of(2, index) + top.shape[0])
    return whole


def plus(*values):
    return sum(v.astype(f32) for v in values).astype(bf16)


class Scatter:
    def __init__(self, terms, x, yh):
        self.terms, self.x, self.yh = terms, x, yh
        self.size, self.n = terms.shape[0] // 8, terms.shape[1]

    def rows(self, k, side, count):
        start = self.size * (2 * ((self.x + k) % 4) + side)
        return lax.dynamic_slice(self.terms, (start, 0), (count * self.size, self.n))

    def first(self, *earlier):
        top, low = after((self.rows(2, 0, 1), self.rows(2, 1, 1)), *earlier)
        self.got = lax.ppermute(top, "x", PLUS), lax.ppermute(low, "x", MINUS)
        return self.got

    def second(self, *earlier):
        from_left, from_right = self.got
        to_right = jnp.concatenate((plus(self.rows(1, 0, 1), from_left), self.rows(1, 1, 1)))
        to_left = jnp.concatenate((self.rows(3, 0, 1), plus(self.rows(3, 1, 1), from_right)))
        to_right, to_left = after((to_right, to_left), *earlier)
        self.got = lax.ppermute(to_right, "x", PLUS), lax.ppermute(to_left, "x", MINUS)
        return self.got

    def last(self, *earlier):
        def mine(side):
            cut = lambda v: lax.dynamic_slice(v, (self.size * side, 0), (self.size, self.n))
            return plus(self.rows(0, side, 1), *(cut(v) for v in self.got))

        sent = lax.ppermute(after(mine(1 - self.yh), *earlier), "yh", SWAP)
        return plus(mine(self.yh), sent)


def body(
    layer_input,
    output_grad,
    expert_ids,
    gate_probs,
    gate_weight,
    up_weight,
    down_weight,
    gate_moment,
    up_moment,
    down_moment,
    gate_second,
    up_second,
    down_second,
):
    x, yh, yl = lax.axis_index("x"), lax.axis_index("yh"), lax.axis_index("yl")
    z, c = lax.axis_index("z"), lax.axis_index("c")
    tok, picks = expert_ids.shape
    capacity = 3 * tok * picks // (2 * GROUPS)
    width = layer_input.shape[1]
    hidden_units = gate_weight.shape[2]
    quarter = hidden_units // 4
    half = hidden_units // 2
    rows = GROUPS * capacity
    depth = gate_weight.shape[1]

    gate_low, up_low = gate_weight[0].astype(bf16), up_weight[0].astype(bf16)

    def chunk(core):
        cuts = [
            w[:, (core + 2 * k) * quarter : (core + 2 * k + 1) * quarter]
            for w in (gate_low, up_low)
            for k in range(2)
        ]
        return jnp.concatenate(cuts, axis=1)

    chunks = (chunk(0), chunk(1))
    part_a = lax.ppermute(jnp.where(yl == 0, chunks[0], chunks[1]), ("yl", "c"), PAIR_A)
    part_b = lax.ppermute(jnp.where(yl == 0, chunks[1], chunks[0]), ("yl", "c"), PAIR_B)
    part = jnp.where(
        c == 0, jnp.concatenate((part_a, part_b)), jnp.concatenate((part_b, part_a))
    )
    down_part = lax.ppermute(down_weight[0].astype(bf16), CYCLE_AXES, CYCLE)

    ids = expert_ids.T
    sent = pack_rows(ids, gate_probs.T.astype(f32), layer_input, output_grad, capacity)
    own = lax.all_to_all(
        sent.reshape(GROUPS, capacity, -1), ("yl", "z"), 0, 0, tiled=True
    ).reshape(rows, -1)

    part_other = lax.ppermute(part, "yh", SWAP)
    down_other = lax.ppermute(down_part, "yh", SWAP)
    near_own = neighbours(part)
    near_other = neighbours(after(part_other, *near_own))
    far_own = far(*near_own, depth)
    far_other = far(*near_other, depth)
    size_down = down_part.shape[0]
    both = jnp.where(
        yh == 0,
        jnp.concatenate((down_part, down_other)),
        jnp.concatenate((down_other, down_part)),
    )
    both = after(both, *near_other, *far_own)
    near_down = neighbours(both)
    far_down = far(*near_down, size_down)
    w_gate_up = place_all(
        2 * depth,
        lambda k, index: 2 * depth * (2 * ((x + k) % 4) + (1 - yh if index else yh)),
        ((part, *near_own, *far_own), (part_other, *near_other, *far_other)),
    )
    w_down = place_all(
        size_down,
        lambda k, index: 2 * size_down * ((x + k) % 4),
        ((both, *near_down, *far_down),),
    )
    other = lax.ppermute(own, "c", SWAP)
    x_rows = jnp.concatenate((own[:, :width], other[:, :width]))
    y_rows = jnp.concatenate((own[:, width : 2 * width], other[:, width : 2 * width]))
    gates = jnp.concatenate((own[:, 2 * width :], other[:, 2 * width :]))[:, :1].astype(f32)

    pre = jnp.dot(x_rows, w_gate_up, preferred_element_type=f32)
    gate_pre, up_pre = pre[:, :half], pre[:, half:]
    sigmoid_gate = jax.nn.sigmoid(gate_pre)
    silu_gate = gate_pre * sigmoid_gate
    hidden_full = silu_gate * up_pre
    hidden = hidden_full.astype(bf16)
    hidden_scaled = (gates * hidden_full).astype(bf16)
    down_term = lax.dot_general(
        hidden_scaled, y_rows, (((0,), (0,)), ((), ())), preferred_element_type=f32
    ).astype(bf16)
    down_sum = Scatter(down_term, x, yh)
    down_sum.first(*near_down)
    down_second_got = down_sum.second(*far_down)
    raw_grad = lax.dot_general(
        y_rows, w_down, (((1,), (1,)), ((), ())), preferred_element_type=f32
    )
    prob_rows = jnp.sum(hidden.astype(f32) * raw_grad, axis=1, keepdims=True)
    hidden_grad = gates * raw_grad
    dsilu = sigmoid_gate * (1.0 + gate_pre * (1.0 - sigmoid_gate))
    pre_grad = jnp.concatenate(
        (hidden_grad * up_pre * dsilu, hidden_grad * silu_gate), axis=1
    ).astype(bf16)
    gate_up_term = lax.dot_general(
        x_rows, pre_grad, (((0,), (0,)), ((), ())), preferred_element_type=f32
    ).astype(bf16)
    gate_up_sum = Scatter(gate_up_term, x, yh)
    gate_up_first = gate_up_sum.first(*down_second_got)
    grad_down = down_sum.last(gate_up_term)
    gate_up_sum.second()
    pre_grad = after(pre_grad, gate_up_term)

    def input_part(d_rows):
        return lax.dot_general(
            d_rows, w_gate_up, (((1,), (1,)), ((), ())), preferred_element_type=f32
        )

    far_rows = lax.ppermute(input_part(pre_grad[rows:]).astype(bf16), "c", SWAP)
    far_prob = lax.ppermute(
        jnp.broadcast_to(prob_rows[rows:], (rows, LANES)), "c", SWAP
    )
    near_rows = (input_part(pre_grad[:rows]) + far_rows.astype(f32)).astype(bf16)
    near_prob = (prob_rows[:rows] + far_prob).astype(bf16)
    packed = jnp.concatenate((near_rows, near_prob), axis=1)
    returned = lax.all_to_all(
        packed.reshape(GROUPS, capacity, -1), ("yl", "z"), 0, 0, tiled=True
    ).reshape(rows, -1)
    input_grad, prob_grad = unpack_rows(ids, returned, width, capacity)

    grad_gate_up = gate_up_sum.last()
    home_a = lax.ppermute(
        lax.dynamic_slice(grad_gate_up, (depth * c, 0), (depth, hidden_units)),
        ("yl", "c"),
        back(PAIR_A),
    ).astype(f32)
    home_b = lax.ppermute(
        lax.dynamic_slice(grad_gate_up, (depth * (1 - c), 0), (depth, hidden_units)),
        ("yl", "c"),
        back(PAIR_B),
    ).astype(f32)
    grad_down = lax.ppermute(grad_down, CYCLE_AXES, back(CYCLE)).astype(f32)
    even = jnp.where(yl == 0, home_a, home_b)
    odd = jnp.where(yl == 0, home_b, home_a)

    def natural(start):
        return jnp.concatenate(
            [
                v[:, start + k * quarter : start + (k + 1) * quarter]
                for k in range(2)
                for v in (even, odd)
            ],
            axis=1,
        )[None]

    new_gate_weight, new_gate_moment, new_gate_second = adamw(
        gate_weight, gate_moment, gate_second, natural(0)
    )
    new_up_weight, new_up_moment, new_up_second = adamw(
        up_weight, up_moment, up_second, natural(half)
    )
    new_down_weight, new_down_moment, new_down_second = adamw(
        down_weight, down_moment, down_second, grad_down[None]
    )
    return (
        input_grad,
        prob_grad.T,
        new_gate_weight,
        new_up_weight,
        new_down_weight,
        new_gate_moment,
        new_up_moment,
        new_down_moment,
        new_gate_second,
        new_up_second,
        new_down_second,
    )


def solution(mesh):
    fine = Mesh(mesh.devices.reshape(4, 2, 2, 4, 2), ("x", "yh", "yl", "z", "c"))
    tokens = P(("x", "yh", "yl", "z", "c"), None)
    weights = P(("z", "c"), ("x", "yh", "yl"), None)
    return jax.shard_map(
        body,
        mesh=fine,
        in_specs=(tokens,) * 4 + (weights,) * 9,
        out_specs=(tokens,) * 2 + (weights,) * 9,
        check_vma=False,
    )
```

```python
import jax
import jax.numpy as jnp
from jax import lax
from jax.experimental import pallas as pl
from jax.experimental.pallas import tpu as pltpu
from jax.sharding import Mesh
from jax.sharding import PartitionSpec as P

beta_one = 0.9
beta_two = 0.95
learn_rate = 0.003
decay_rate = 0.1
epsilon = 1e-08
correct_one = 1.0 - 2.6561398887587e-05
correct_two = 1.0 - 0.005920529220333

LANES = 128
GROUPS = 8
f32 = jnp.float32
bf16 = jnp.bfloat16

PLUS = [(i, (i + 1) % 4) for i in range(4)]
MINUS = [(i, (i - 1) % 4) for i in range(4)]
SWAP = [(0, 1), (1, 0)]
PAIR_A = [(2 * yl + c, 2 * c + yl) for yl in range(2) for c in range(2)]
PAIR_B = [(2 * yl + c, 2 * c + 1 - yl) for yl in range(2) for c in range(2)]


def _cycle():
    pairs = []
    for x1 in range(2):
        for x0 in range(2):
            for yh in range(2):
                for yl in range(2):
                    for c in range(2):
                        src = (((x1 * 2 + x0) * 2 + yh) * 2 + yl) * 2 + c
                        dst = (((x1 * 2 + yh) * 2 + yl) * 2 + c) * 2 + x0
                        pairs.append((src, dst))
    return pairs


CYCLE = _cycle()
CYCLE_AXES = ("x", "yh", "yl", "c")


def back(pairs):
    return [(d, s) for s, d in pairs]


def after(value, *earlier):
    return lax.optimization_barrier((value, earlier))[0]


join = lax.optimization_barrier


def adamw(weight, moment, second, grad):
    moment_new = beta_one * moment + (1.0 - beta_one) * grad
    second_new = beta_two * second + (1.0 - beta_two) * grad * grad
    update = moment_new / correct_one / (jnp.sqrt(second_new / correct_two) + epsilon)
    return (weight - learn_rate * (update + decay_rate * weight), moment_new, second_new)


def one_hots(ids, capacity):
    tok = ids.shape[1]
    experts = lax.broadcasted_iota(jnp.int32, (GROUPS, tok), 0)
    named = [(experts == ids[k : k + 1, :]).astype(f32) for k in range(2)]
    earlier = (
        lax.broadcasted_iota(jnp.int32, (tok, tok), 0)
        < lax.broadcasted_iota(jnp.int32, (tok, tok), 1)
    ).astype(f32)
    count = jnp.dot(
        (named[0] + named[1]).astype(bf16), earlier.astype(bf16), preferred_element_type=f32
    )
    slot = lax.broadcasted_iota(jnp.int32, (GROUPS * capacity, tok), 0)
    hots = []
    for k in range(2):
        rank = jnp.sum(named[k] * count, axis=0, keepdims=True).astype(jnp.int32)
        expert = ids[k : k + 1, :]
        dest = ((expert & 1) * 4 + (expert >> 1)) * capacity + rank
        hots.append((slot == dest).astype(f32))
    return hots


def block_of(width):
    return 512 if width % 512 == 0 else width


def pack_kernel(capacity, width, ids_ref, probs_ref, x_ref, y_ref, out_ref):
    first, second = one_hots(ids_ref[...], capacity)
    hot = (first + second).astype(bf16)
    probs = probs_ref[...]
    gates = (first * probs[0:1, :] + second * probs[1:2, :]).astype(bf16)
    ones = jnp.ones((gates.shape[1], LANES), bf16)
    out_ref[:, 2 * width :] = jnp.dot(gates, ones, preferred_element_type=f32).astype(bf16)
    block = block_of(width)

    def step(i, carry):
        at = pl.multiple_of(i * block, block)
        cols = pl.ds(at, block)
        out_ref[:, cols] = jnp.dot(
            hot, x_ref[:, cols], preferred_element_type=f32
        ).astype(bf16)
        out_ref[:, pl.ds(pl.multiple_of(at + width, block), block)] = jnp.dot(
            hot, y_ref[:, cols], preferred_element_type=f32
        ).astype(bf16)
        return carry

    lax.fori_loop(0, width // block, step, 0)


def unpack_kernel(capacity, width, ids_ref, rows_ref, x_ref, prob_ref):
    first, second = one_hots(ids_ref[...], capacity)
    hot = (first + second).astype(bf16)
    block = block_of(width)

    def step(i, carry):
        cols = pl.ds(pl.multiple_of(i * block, block), block)
        x_ref[:, cols] = lax.dot_general(
            hot, rows_ref[:, cols], (((0,), (0,)), ((), ())), preferred_element_type=f32
        ).astype(bf16)
        return carry

    lax.fori_loop(0, width // block, step, 0)
    q_col = rows_ref[:, width:].astype(f32)
    prob_ref[0:1, :] = jnp.sum(first * q_col, axis=0, keepdims=True).astype(bf16)
    prob_ref[1:2, :] = jnp.sum(second * q_col, axis=0, keepdims=True).astype(bf16)


def vmem_specs(count):
    return [pl.BlockSpec(memory_space=pltpu.VMEM) for _ in range(count)]


def pack_rows(ids, probs, x, y, capacity):
    width = x.shape[1]
    return pl.pallas_call(
        lambda *refs: pack_kernel(capacity, width, *refs),
        out_shape=jax.ShapeDtypeStruct((GROUPS * capacity, 2 * width + LANES), bf16),
        in_specs=vmem_specs(4),
        out_specs=vmem_specs(1)[0],
        compiler_params=pltpu.CompilerParams(vmem_limit_bytes=40 << 20),
        name="pack_rows",
    )(ids, probs, x, y)


def unpack_rows(ids, rows, width, capacity):
    tok = ids.shape[1]
    return pl.pallas_call(
        lambda *refs: unpack_kernel(capacity, width, *refs),
        out_shape=(
            jax.ShapeDtypeStruct((tok, width), bf16),
            jax.ShapeDtypeStruct((2, tok), bf16),
        ),
        in_specs=vmem_specs(2),
        out_specs=tuple(vmem_specs(2)),
        compiler_params=pltpu.CompilerParams(vmem_limit_bytes=40 << 20),
        name="unpack_rows",
    )(ids, rows)


def put(whole, part, row):
    return lax.dynamic_update_slice(whole, part, (row, 0))


def neighbours(part):
    return lax.ppermute(part, "x", PLUS), lax.ppermute(part, "x", MINUS)


def far(left, right, half):
    return lax.ppermute(left[:half], "x", PLUS), lax.ppermute(right[half:], "x", MINUS)


def place_all(size, rows_of, sets):
    whole = jnp.zeros((8 * size, sets[0][0].shape[1]), bf16)
    for index, (part, left, right, top, low) in enumerate(sets):
        whole = put(whole, part, rows_of(0, index))
        whole = put(whole, left, rows_of(3, index))
        whole = put(whole, right, rows_of(1, index))
        whole = put(whole, top, rows_of(2, index))
        whole = put(whole, low, rows_of(2, index) + top.shape[0])
    return whole


def plus(*values):
    return sum(v.astype(f32) for v in values).astype(bf16)


class Scatter:
    def __init__(self, terms, x, yh):
        self.terms, self.x, self.yh = terms, x, yh
        self.size, self.n = terms.shape[0] // 8, terms.shape[1]

    def rows(self, k, side, count):
        start = self.size * (2 * ((self.x + k) % 4) + side)
        return lax.dynamic_slice(self.terms, (start, 0), (count * self.size, self.n))

    def first(self):
        top, low = self.rows(2, 0, 1), self.rows(2, 1, 1)
        return lax.ppermute(top, "x", PLUS), lax.ppermute(low, "x", MINUS)

    def second(self, got):
        from_left, from_right = got
        to_right = jnp.concatenate((plus(self.rows(1, 0, 1), from_left), self.rows(1, 1, 1)))
        to_left = jnp.concatenate((self.rows(3, 0, 1), plus(self.rows(3, 1, 1), from_right)))
        return lax.ppermute(to_right, "x", PLUS), lax.ppermute(to_left, "x", MINUS)

    def mine(self, side):
        cut = lambda v: lax.dynamic_slice(v, (self.size * side, 0), (self.size, self.n))
        return plus(self.rows(0, side, 1), *(cut(v) for v in self.got))

    def third(self):
        self.kept = self.mine(self.yh)
        return lax.ppermute(self.mine(1 - self.yh), "yh", SWAP)

    def last(self, sent):
        return plus(self.kept, sent)


def body(
    layer_input,
    output_grad,
    expert_ids,
    gate_probs,
    gate_weight,
    up_weight,
    down_weight,
    gate_moment,
    up_moment,
    down_moment,
    gate_second,
    up_second,
    down_second,
):
    x, yh, yl = lax.axis_index("x"), lax.axis_index("yh"), lax.axis_index("yl")
    z, c = lax.axis_index("z"), lax.axis_index("c")
    tok, picks = expert_ids.shape
    capacity = 3 * tok * picks // (2 * GROUPS)
    width = layer_input.shape[1]
    hidden_units = gate_weight.shape[2]
    quarter = hidden_units // 4
    half = hidden_units // 2
    rows = GROUPS * capacity
    depth = gate_weight.shape[1]

    gate_low, up_low = gate_weight[0].astype(bf16), up_weight[0].astype(bf16)

    def chunk(core):
        cuts = [
            w[:, (core + 2 * k) * quarter : (core + 2 * k + 1) * quarter]
            for w in (gate_low, up_low)
            for k in range(2)
        ]
        return jnp.concatenate(cuts, axis=1)

    chunks = (chunk(0), chunk(1))
    part_a = lax.ppermute(jnp.where(yl == 0, chunks[0], chunks[1]), ("yl", "c"), PAIR_A)
    part_b = lax.ppermute(jnp.where(yl == 0, chunks[1], chunks[0]), ("yl", "c"), PAIR_B)
    part = jnp.where(
        c == 0, jnp.concatenate((part_a, part_b)), jnp.concatenate((part_b, part_a))
    )
    down_part = lax.ppermute(down_weight[0].astype(bf16), CYCLE_AXES, CYCLE)

    part_other = lax.ppermute(part, "yh", SWAP)
    near_own = neighbours(part)
    part_other, near_own, down_part = join((part_other, near_own, down_part))

    down_other = lax.ppermute(down_part, "yh", SWAP)
    near_other = neighbours(part_other)
    far_own = far(*near_own, depth)
    ids = expert_ids.T
    sent = pack_rows(ids, gate_probs.T.astype(f32), layer_input, output_grad, capacity)
    own = lax.all_to_all(
        after(sent, part_other).reshape(GROUPS, capacity, -1), ("yl", "z"), 0, 0, tiled=True
    ).reshape(rows, -1)
    down_other, near_other, far_own = join((down_other, near_other, far_own))

    size_down = down_part.shape[0]
    both = jnp.where(
        yh == 0,
        jnp.concatenate((down_part, down_other)),
        jnp.concatenate((down_other, down_part)),
    )
    near_down = neighbours(both)
    far_other = far(*near_other, depth)
    near_down, far_other = join((near_down, far_other))
    far_down = far(*near_down, size_down)
    w_gate_up = place_all(
        2 * depth,
        lambda k, index: 2 * depth * (2 * ((x + k) % 4) + (1 - yh if index else yh)),
        ((part, *near_own, *far_own), (part_other, *near_other, *far_other)),
    )
    w_down = place_all(
        size_down,
        lambda k, index: 2 * size_down * ((x + k) % 4),
        ((both, *near_down, *far_down),),
    )
    other = lax.ppermute(own, "c", SWAP)
    x_rows = jnp.concatenate((own[:, :width], other[:, :width]))
    y_rows = jnp.concatenate((own[:, width : 2 * width], other[:, width : 2 * width]))
    gates = jnp.concatenate((own[:, 2 * width :], other[:, 2 * width :]))[:, :1].astype(f32)

    pre = jnp.dot(x_rows, w_gate_up, preferred_element_type=f32)
    gate_pre, up_pre = pre[:, :half], pre[:, half:]
    sigmoid_gate = jax.nn.sigmoid(gate_pre)
    silu_gate = gate_pre * sigmoid_gate
    hidden_full = silu_gate * up_pre
    hidden = hidden_full.astype(bf16)
    hidden_scaled = (gates * hidden_full).astype(bf16)
    down_term = lax.dot_general(
        hidden_scaled, y_rows, (((0,), (0,)), ((), ())), preferred_element_type=f32
    ).astype(bf16)
    down_sum = Scatter(down_term, x, yh)
    down_got = down_sum.second(down_sum.first())
    raw_grad = lax.dot_general(
        y_rows, w_down, (((1,), (1,)), ((), ())), preferred_element_type=f32
    )
    prob_rows = jnp.sum(hidden.astype(f32) * raw_grad, axis=1, keepdims=True)
    hidden_grad = gates * raw_grad
    dsilu = sigmoid_gate * (1.0 + gate_pre * (1.0 - sigmoid_gate))
    gate_grad = (hidden_grad * up_pre * dsilu).astype(bf16)
    up_grad = (hidden_grad * silu_gate).astype(bf16)

    def x_term(d_rows):
        return lax.dot_general(
            x_rows, d_rows, (((0,), (0,)), ((), ())), preferred_element_type=f32
        ).astype(bf16)

    gate_term = x_term(gate_grad)
    gate_sum = Scatter(gate_term, x, yh)
    gate_got = gate_sum.first()
    up_term = x_term(after(up_grad, gate_term))
    up_sum = Scatter(up_term, x, yh)
    pre_grad = after(jnp.concatenate((gate_grad, up_grad), axis=1), up_term)

    def input_part(d_rows):
        return lax.dot_general(
            d_rows, w_gate_up, (((1,), (1,)), ((), ())), preferred_element_type=f32
        )

    far_rows = lax.ppermute(input_part(pre_grad[rows:]).astype(bf16), "c", SWAP)
    far_prob = lax.ppermute(
        jnp.broadcast_to(prob_rows[rows:], (rows, LANES)), "c", SWAP
    )
    near_rows = (input_part(pre_grad[:rows]) + far_rows.astype(f32)).astype(bf16)
    near_prob = (prob_rows[:rows] + far_prob).astype(bf16)
    packed = jnp.concatenate((near_rows, near_prob), axis=1)
    packed, gate_got, down_sum.got = join((packed, gate_got, down_got))
    gate_got = gate_sum.second(gate_got)
    up_got = up_sum.first()
    down_sent = down_sum.third()
    up_got, gate_sum.got, down_sent = join((up_got, gate_got, down_sent))
    returned = lax.all_to_all(
        packed.reshape(GROUPS, capacity, -1), ("yl", "z"), 0, 0, tiled=True
    ).reshape(rows, -1)
    def send_home(grad):
        return tuple(
            lax.ppermute(
                lax.dynamic_slice(grad, (depth * start, 0), (depth, half)),
                ("yl", "c"),
                back(pairs),
            )
            for start, pairs in ((c, PAIR_A), (1 - c, PAIR_B))
        )

    def natural(home):
        even = jnp.where(yl == 0, home[0], home[1])
        odd = jnp.where(yl == 0, home[1], home[0])
        return jnp.concatenate(
            [v[:, k * quarter : (k + 1) * quarter] for k in range(2) for v in (even, odd)],
            axis=1,
        )[None].astype(f32)

    down_home = lax.ppermute(down_sum.last(down_sent), CYCLE_AXES, back(CYCLE))
    up_got = up_sum.second(up_got)
    gate_sent = gate_sum.third()
    up_sum.got, gate_sent, down_home, returned = join((up_got, gate_sent, down_home, returned))
    up_sent = up_sum.third()
    gate_home = send_home(gate_sum.last(gate_sent))
    input_grad, prob_grad = unpack_rows(ids, returned, width, capacity)
    new_down_weight, new_down_moment, new_down_second = adamw(
        down_weight, down_moment, down_second, down_home.astype(f32)[None]
    )
    up_sent, gate_home = join((up_sent, gate_home))
    up_home = send_home(up_sum.last(up_sent))
    new_gate_weight, new_gate_moment, new_gate_second = adamw(
        gate_weight, gate_moment, gate_second, natural(gate_home)
    )
    new_up_weight, new_up_moment, new_up_second = adamw(
        up_weight, up_moment, up_second, natural(after(up_home, new_gate_weight))
    )
    return (
        input_grad,
        prob_grad.T,
        new_gate_weight,
        new_up_weight,
        new_down_weight,
        new_gate_moment,
        new_up_moment,
        new_down_moment,
        new_gate_second,
        new_up_second,
        new_down_second,
    )


def solution(mesh):
    fine = Mesh(mesh.devices.reshape(4, 2, 2, 4, 2), ("x", "yh", "yl", "z", "c"))
    tokens = P(("x", "yh", "yl", "z", "c"), None)
    weights = P(("z", "c"), ("x", "yh", "yl"), None)
    return jax.shard_map(
        body,
        mesh=fine,
        in_specs=(tokens,) * 4 + (weights,) * 9,
        out_specs=(tokens,) * 2 + (weights,) * 9,
        check_vma=False,
    )
```

```python
import jax
import jax.numpy as jnp
from jax import lax
from jax.experimental import pallas as pl
from jax.experimental.pallas import tpu as pltpu
from jax.sharding import Mesh
from jax.sharding import PartitionSpec as P

beta_one = 0.9
beta_two = 0.95
learn_rate = 0.003
decay_rate = 0.1
epsilon = 1e-08
correct_one = 1.0 - 2.6561398887587e-05
correct_two = 1.0 - 0.005920529220333

LANES = 128
GROUPS = 8
f32 = jnp.float32
bf16 = jnp.bfloat16

PLUS = [(i, (i + 1) % 4) for i in range(4)]
MINUS = [(i, (i - 1) % 4) for i in range(4)]
SWAP = [(0, 1), (1, 0)]
PAIR_A = [(2 * yl + c, 2 * c + yl) for yl in range(2) for c in range(2)]
PAIR_B = [(2 * yl + c, 2 * c + 1 - yl) for yl in range(2) for c in range(2)]


def _cycle():
    pairs = []
    for x1 in range(2):
        for x0 in range(2):
            for yh in range(2):
                for yl in range(2):
                    for c in range(2):
                        src = (((x1 * 2 + x0) * 2 + yh) * 2 + yl) * 2 + c
                        dst = (((x1 * 2 + yh) * 2 + yl) * 2 + c) * 2 + x0
                        pairs.append((src, dst))
    return pairs


CYCLE = _cycle()
CYCLE_AXES = ("x", "yh", "yl", "c")


def back(pairs):
    return [(d, s) for s, d in pairs]


join = lax.optimization_barrier


def adamw(weight, moment, second, grad):
    moment_new = beta_one * moment + (1.0 - beta_one) * grad
    second_new = beta_two * second + (1.0 - beta_two) * grad * grad
    update = moment_new / correct_one / (jnp.sqrt(second_new / correct_two) + epsilon)
    return (weight - learn_rate * (update + decay_rate * weight), moment_new, second_new)


def one_hots(ids, capacity):
    tok = ids.shape[1]
    experts = lax.broadcasted_iota(jnp.int32, (GROUPS, tok), 0)
    named = [(experts == ids[k : k + 1, :]).astype(f32) for k in range(2)]
    earlier = (
        lax.broadcasted_iota(jnp.int32, (tok, tok), 0)
        < lax.broadcasted_iota(jnp.int32, (tok, tok), 1)
    ).astype(f32)
    count = jnp.dot(
        (named[0] + named[1]).astype(bf16), earlier.astype(bf16), preferred_element_type=f32
    )
    slot = lax.broadcasted_iota(jnp.int32, (GROUPS * capacity, tok), 0)
    hots = []
    for k in range(2):
        rank = jnp.sum(named[k] * count, axis=0, keepdims=True).astype(jnp.int32)
        expert = ids[k : k + 1, :]
        dest = ((expert & 1) * 4 + (expert >> 1)) * capacity + rank
        hots.append((slot == dest).astype(f32))
    return hots


def block_of(width):
    return 512 if width % 512 == 0 else width


def pack_kernel(capacity, width, ids_ref, probs_ref, x_ref, y_ref, out_ref):
    first, second = one_hots(ids_ref[...], capacity)
    hot = (first + second).astype(bf16)
    probs = probs_ref[...]
    gates = (first * probs[0:1, :] + second * probs[1:2, :]).astype(bf16)
    ones = jnp.ones((gates.shape[1], LANES), bf16)
    out_ref[:, 2 * width :] = jnp.dot(gates, ones, preferred_element_type=f32).astype(bf16)
    block = block_of(width)

    def step(i, carry):
        at = pl.multiple_of(i * block, block)
        cols = pl.ds(at, block)
        out_ref[:, cols] = jnp.dot(
            hot, x_ref[:, cols], preferred_element_type=f32
        ).astype(bf16)
        out_ref[:, pl.ds(pl.multiple_of(at + width, block), block)] = jnp.dot(
            hot, y_ref[:, cols], preferred_element_type=f32
        ).astype(bf16)
        return carry

    lax.fori_loop(0, width // block, step, 0)


def unpack_kernel(capacity, width, ids_ref, rows_ref, x_ref, prob_ref):
    first, second = one_hots(ids_ref[...], capacity)
    hot = (first + second).astype(bf16)
    block = block_of(width)

    def step(i, carry):
        cols = pl.ds(pl.multiple_of(i * block, block), block)
        x_ref[:, cols] = lax.dot_general(
            hot, rows_ref[:, cols], (((0,), (0,)), ((), ())), preferred_element_type=f32
        ).astype(bf16)
        return carry

    lax.fori_loop(0, width // block, step, 0)
    q_col = rows_ref[:, width:].astype(f32)
    prob_ref[0:1, :] = jnp.sum(first * q_col, axis=0, keepdims=True).astype(bf16)
    prob_ref[1:2, :] = jnp.sum(second * q_col, axis=0, keepdims=True).astype(bf16)


def vmem_specs(count):
    return [pl.BlockSpec(memory_space=pltpu.VMEM) for _ in range(count)]


def pack_rows(ids, probs, x, y, capacity):
    width = x.shape[1]
    return pl.pallas_call(
        lambda *refs: pack_kernel(capacity, width, *refs),
        out_shape=jax.ShapeDtypeStruct((GROUPS * capacity, 2 * width + LANES), bf16),
        in_specs=vmem_specs(4),
        out_specs=vmem_specs(1)[0],
        compiler_params=pltpu.CompilerParams(vmem_limit_bytes=40 << 20),
        name="pack_rows",
    )(ids, probs, x, y)


def unpack_rows(ids, rows, width, capacity):
    tok = ids.shape[1]
    return pl.pallas_call(
        lambda *refs: unpack_kernel(capacity, width, *refs),
        out_shape=(
            jax.ShapeDtypeStruct((tok, width), bf16),
            jax.ShapeDtypeStruct((2, tok), bf16),
        ),
        in_specs=vmem_specs(2),
        out_specs=tuple(vmem_specs(2)),
        compiler_params=pltpu.CompilerParams(vmem_limit_bytes=40 << 20),
        name="unpack_rows",
    )(ids, rows)


def put(whole, part, row):
    return lax.dynamic_update_slice(whole, part, (row, 0))


def neighbours(part):
    return lax.ppermute(part, "x", PLUS), lax.ppermute(part, "x", MINUS)


def far(left, right, half):
    return lax.ppermute(left[:half], "x", PLUS), lax.ppermute(right[half:], "x", MINUS)


def place_all(size, rows_of, sets):
    whole = jnp.zeros((8 * size, sets[0][0].shape[1]), bf16)
    for index, (part, left, right, top, low) in enumerate(sets):
        whole = put(whole, part, rows_of(0, index))
        whole = put(whole, left, rows_of(3, index))
        whole = put(whole, right, rows_of(1, index))
        whole = put(whole, top, rows_of(2, index))
        whole = put(whole, low, rows_of(2, index) + top.shape[0])
    return whole


def plus(*values):
    return sum(v.astype(f32) for v in values).astype(bf16)


def send(pair):
    to_right, to_left = pair
    return lax.ppermute(to_right, "x", PLUS), lax.ppermute(to_left, "x", MINUS)


class Scatter:
    def __init__(self, terms, x, yh):
        self.terms, self.x, self.yh = terms, x, yh
        self.size, self.n = terms.shape[0] // 8, terms.shape[1]

    def rows(self, k, side, count):
        start = self.size * (2 * ((self.x + k) % 4) + side)
        return lax.dynamic_slice(self.terms, (start, 0), (count * self.size, self.n))

    def first(self):
        to_right = jnp.concatenate((self.rows(2, 0, 1), self.rows(1, 1, 1)))
        to_left = jnp.concatenate((self.rows(2, 1, 1), self.rows(3, 0, 1)))
        return to_right, to_left

    def second(self, got):
        from_left, from_right = got
        self.low, self.top = from_left[self.size :], from_right[self.size :]
        to_right = plus(self.rows(1, 0, 1), from_left[: self.size])
        to_left = plus(self.rows(3, 1, 1), from_right[: self.size])
        return to_right, to_left

    def mine(self, side):
        top, low = self.got
        return plus(
            self.rows(0, side, 1),
            jnp.where(side == 0, top, self.low),
            jnp.where(side == 0, self.top, low),
        )

    def third(self):
        self.kept = self.mine(self.yh)
        return lax.ppermute(self.mine(1 - self.yh), "yh", SWAP)

    def last(self, sent):
        return plus(self.kept, sent)


def body(
    layer_input,
    output_grad,
    expert_ids,
    gate_probs,
    gate_weight,
    up_weight,
    down_weight,
    gate_moment,
    up_moment,
    down_moment,
    gate_second,
    up_second,
    down_second,
):
    x, yh, yl = lax.axis_index("x"), lax.axis_index("yh"), lax.axis_index("yl")
    z, c = lax.axis_index("z"), lax.axis_index("c")
    tok, picks = expert_ids.shape
    capacity = 3 * tok * picks // (2 * GROUPS)
    width = layer_input.shape[1]
    hidden_units = gate_weight.shape[2]
    quarter = hidden_units // 4
    half = hidden_units // 2
    rows = GROUPS * capacity
    depth = gate_weight.shape[1]

    gate_low, up_low = gate_weight[0].astype(bf16), up_weight[0].astype(bf16)

    def chunk(core):
        cuts = [
            w[:, (core + 2 * k) * quarter : (core + 2 * k + 1) * quarter]
            for w in (gate_low, up_low)
            for k in range(2)
        ]
        return jnp.concatenate(cuts, axis=1)

    chunks = (chunk(0), chunk(1))
    part_a = lax.ppermute(jnp.where(yl == 0, chunks[0], chunks[1]), ("yl", "c"), PAIR_A)
    part_b = lax.ppermute(jnp.where(yl == 0, chunks[1], chunks[0]), ("yl", "c"), PAIR_B)
    part = jnp.where(
        c == 0, jnp.concatenate((part_a, part_b)), jnp.concatenate((part_b, part_a))
    )
    down_part = lax.ppermute(down_weight[0].astype(bf16), CYCLE_AXES, CYCLE)

    part_other = lax.ppermute(part, "yh", SWAP)
    down_other = lax.ppermute(down_part, "yh", SWAP)
    near_own = join(neighbours(part))
    far_own = far(*near_own, depth)
    part_other, down_other, far_own = join((part_other, down_other, far_own))

    size_down = down_part.shape[0]
    both = jnp.where(
        yh == 0,
        jnp.concatenate((down_part, down_other)),
        jnp.concatenate((down_other, down_part)),
    )
    ids = expert_ids.T
    sent = pack_rows(ids, gate_probs.T.astype(f32), layer_input, output_grad, capacity)
    sent, both, part_other = join((sent, both, part_other))
    near_other = neighbours(part_other)
    near_down = neighbours(both)
    own = lax.all_to_all(
        sent.reshape(GROUPS, capacity, -1), ("yl", "z"), 0, 0, tiled=True
    ).reshape(rows, -1)
    near_other, near_down = join((near_other, near_down))
    far_other = far(*near_other, depth)
    far_down = far(*near_down, size_down)
    own, far_other, far_down = join((own, far_other, far_down))
    w_gate_up = place_all(
        2 * depth,
        lambda k, index: 2 * depth * (2 * ((x + k) % 4) + (1 - yh if index else yh)),
        ((part, *near_own, *far_own), (part_other, *near_other, *far_other)),
    )
    other = lax.ppermute(own, "c", SWAP)
    x_rows = jnp.concatenate((own[:, :width], other[:, :width]))
    y_rows = jnp.concatenate((own[:, width : 2 * width], other[:, width : 2 * width]))
    gates = jnp.concatenate((own[:, 2 * width :], other[:, 2 * width :]))[:, :1].astype(f32)

    pre = jnp.dot(x_rows, w_gate_up, preferred_element_type=f32)
    gate_pre, up_pre = pre[:, :half], pre[:, half:]
    sigmoid_gate = jax.nn.sigmoid(gate_pre)
    silu_gate = gate_pre * sigmoid_gate
    hidden_full = silu_gate * up_pre
    hidden = hidden_full.astype(bf16)
    hidden_scaled = (gates * hidden_full).astype(bf16)
    down_term = lax.dot_general(
        hidden_scaled, y_rows, (((0,), (0,)), ((), ())), preferred_element_type=f32
    ).astype(bf16)
    down_sum = Scatter(down_term, x, yh)
    down_send = down_sum.first()
    w_down = place_all(
        size_down,
        lambda k, index: 2 * size_down * ((x + k) % 4),
        ((both, *near_down, *far_down),),
    )
    down_send, w_down = join((down_send, w_down))
    down_got = send(down_send)
    raw_grad = lax.dot_general(
        y_rows, w_down, (((1,), (1,)), ((), ())), preferred_element_type=f32
    )
    prob_rows = jnp.sum(hidden.astype(f32) * raw_grad, axis=1, keepdims=True)
    hidden_grad = gates * raw_grad
    dsilu = sigmoid_gate * (1.0 + gate_pre * (1.0 - sigmoid_gate))
    gate_grad = (hidden_grad * up_pre * dsilu).astype(bf16)
    up_grad = (hidden_grad * silu_gate).astype(bf16)

    def x_term(d_rows):
        return lax.dot_general(
            x_rows, d_rows, (((0,), (0,)), ((), ())), preferred_element_type=f32
        ).astype(bf16)

    gate_term = x_term(gate_grad)
    gate_term, up_grad = join((gate_term, up_grad))
    up_term = x_term(up_grad)
    up_term, pre_grad = join((up_term, jnp.concatenate((gate_grad, up_grad), axis=1)))
    gate_sum, up_sum = Scatter(gate_term, x, yh), Scatter(up_term, x, yh)

    def input_part(d_rows):
        return lax.dot_general(
            d_rows, w_gate_up, (((1,), (1,)), ((), ())), preferred_element_type=f32
        )

    far_part = input_part(pre_grad[rows:]).astype(bf16)
    far_prob = jnp.broadcast_to(prob_rows[rows:], (rows, LANES))
    down_got, far_part = join((down_got, far_part))
    far_rows = lax.ppermute(far_part, "c", SWAP)
    far_prob = lax.ppermute(far_prob, "c", SWAP)
    down_send = down_sum.second(down_got)
    gate_send = gate_sum.first()
    pre_grad, down_send, gate_send = join((pre_grad, down_send, gate_send))
    down_got, gate_got = send(down_send), send(gate_send)
    near_rows = (input_part(pre_grad[:rows]) + far_rows.astype(f32)).astype(bf16)
    near_prob = (prob_rows[:rows] + far_prob).astype(bf16)
    packed = jnp.concatenate((near_rows, near_prob), axis=1)
    packed, gate_got, down_sum.got = join((packed, gate_got, down_got))
    gate_send, up_send = join((gate_sum.second(gate_got), up_sum.first()))
    gate_got, up_got = send(gate_send), send(up_send)
    down_sent = down_sum.third()
    up_got, gate_sum.got, down_sent = join((up_got, gate_got, down_sent))
    returned = lax.all_to_all(
        packed.reshape(GROUPS, capacity, -1), ("yl", "z"), 0, 0, tiled=True
    ).reshape(rows, -1)
    def send_home(grad):
        return tuple(
            lax.ppermute(
                lax.dynamic_slice(grad, (depth * start, 0), (depth, half)),
                ("yl", "c"),
                back(pairs),
            )
            for start, pairs in ((c, PAIR_A), (1 - c, PAIR_B))
        )

    def natural(home):
        even = jnp.where(yl == 0, home[0], home[1])
        odd = jnp.where(yl == 0, home[1], home[0])
        return jnp.concatenate(
            [v[:, k * quarter : (k + 1) * quarter] for k in range(2) for v in (even, odd)],
            axis=1,
        )[None].astype(f32)

    down_home = lax.ppermute(down_sum.last(down_sent), CYCLE_AXES, back(CYCLE))
    up_got = send(up_sum.second(up_got))
    gate_sent = gate_sum.third()
    up_sum.got, gate_sent, down_home, returned = join((up_got, gate_sent, down_home, returned))
    up_sent = up_sum.third()
    gate_home = send_home(gate_sum.last(gate_sent))
    new_down_weight, new_down_moment, new_down_second = adamw(
        down_weight, down_moment, down_second, down_home.astype(f32)[None]
    )
    up_sent, gate_home = join((up_sent, gate_home))
    up_home = send_home(up_sum.last(up_sent))
    input_grad, prob_grad = unpack_rows(ids, returned, width, capacity)
    new_gate_weight, new_gate_moment, new_gate_second = adamw(
        gate_weight, gate_moment, gate_second, natural(gate_home)
    )
    up_home, new_gate_weight = join((up_home, new_gate_weight))
    new_up_weight, new_up_moment, new_up_second = adamw(
        up_weight, up_moment, up_second, natural(up_home)
    )
    return (
        input_grad,
        prob_grad.T,
        new_gate_weight,
        new_up_weight,
        new_down_weight,
        new_gate_moment,
        new_up_moment,
        new_down_moment,
        new_gate_second,
        new_up_second,
        new_down_second,
    )


def solution(mesh):
    fine = Mesh(mesh.devices.reshape(4, 2, 2, 4, 2), ("x", "yh", "yl", "z", "c"))
    tokens = P(("x", "yh", "yl", "z", "c"), None)
    weights = P(("z", "c"), ("x", "yh", "yl"), None)
    return jax.shard_map(
        body,
        mesh=fine,
        in_specs=(tokens,) * 4 + (weights,) * 9,
        out_specs=(tokens,) * 2 + (weights,) * 9,
        check_vma=False,
    )
```

```python
import jax
import jax.numpy as jnp
from jax import lax
from jax.experimental import pallas as pl
from jax.experimental.pallas import tpu as pltpu
from jax.sharding import Mesh
from jax.sharding import PartitionSpec as P

beta_one = 0.9
beta_two = 0.95
learn_rate = 0.003
decay_rate = 0.1
epsilon = 1e-08
correct_one = 1.0 - 2.6561398887587e-05
correct_two = 1.0 - 0.005920529220333

LANES = 128
GROUPS = 8
f32 = jnp.float32
bf16 = jnp.bfloat16

PLUS = [(i, (i + 1) % 4) for i in range(4)]
MINUS = [(i, (i - 1) % 4) for i in range(4)]
SWAP = [(0, 1), (1, 0)]
PAIR_A = [(2 * yl + c, 2 * c + yl) for yl in range(2) for c in range(2)]
PAIR_B = [(2 * yl + c, 2 * c + 1 - yl) for yl in range(2) for c in range(2)]


def _cycle():
    pairs = []
    for x1 in range(2):
        for x0 in range(2):
            for yh in range(2):
                for yl in range(2):
                    for c in range(2):
                        src = (((x1 * 2 + x0) * 2 + yh) * 2 + yl) * 2 + c
                        dst = (((x1 * 2 + yh) * 2 + yl) * 2 + c) * 2 + x0
                        pairs.append((src, dst))
    return pairs


CYCLE = _cycle()
CYCLE_AXES = ("x", "yh", "yl", "c")


def back(pairs):
    return [(d, s) for s, d in pairs]


join = lax.optimization_barrier


def adamw(weight, moment, second, grad):
    moment_new = beta_one * moment + (1.0 - beta_one) * grad
    second_new = beta_two * second + (1.0 - beta_two) * grad * grad
    update = moment_new / correct_one / (jnp.sqrt(second_new / correct_two) + epsilon)
    return (weight - learn_rate * (update + decay_rate * weight), moment_new, second_new)


def one_hots(ids, capacity):
    tok = ids.shape[1]
    experts = lax.broadcasted_iota(jnp.int32, (GROUPS, tok), 0)
    named = [(experts == ids[k : k + 1, :]).astype(f32) for k in range(2)]
    earlier = (
        lax.broadcasted_iota(jnp.int32, (tok, tok), 0)
        < lax.broadcasted_iota(jnp.int32, (tok, tok), 1)
    ).astype(f32)
    count = jnp.dot(
        (named[0] + named[1]).astype(bf16), earlier.astype(bf16), preferred_element_type=f32
    )
    slot = lax.broadcasted_iota(jnp.int32, (GROUPS * capacity, tok), 0)
    hots = []
    for k in range(2):
        rank = jnp.sum(named[k] * count, axis=0, keepdims=True).astype(jnp.int32)
        expert = ids[k : k + 1, :]
        dest = ((expert & 1) * 4 + (expert >> 1)) * capacity + rank
        hots.append((slot == dest).astype(f32))
    return hots


def block_of(width):
    return 512 if width % 512 == 0 else width


def pack_kernel(capacity, width, ids_ref, probs_ref, x_ref, y_ref, out_ref):
    first, second = one_hots(ids_ref[...], capacity)
    hot = (first + second).astype(bf16)
    probs = probs_ref[...]
    gates = (first * probs[0:1, :] + second * probs[1:2, :]).astype(bf16)
    ones = jnp.ones((gates.shape[1], LANES), bf16)
    out_ref[:, 2 * width :] = jnp.dot(gates, ones, preferred_element_type=f32).astype(bf16)
    block = block_of(width)

    def step(i, carry):
        at = pl.multiple_of(i * block, block)
        cols = pl.ds(at, block)
        out_ref[:, cols] = jnp.dot(
            hot, x_ref[:, cols], preferred_element_type=f32
        ).astype(bf16)
        out_ref[:, pl.ds(pl.multiple_of(at + width, block), block)] = jnp.dot(
            hot, y_ref[:, cols], preferred_element_type=f32
        ).astype(bf16)
        return carry

    lax.fori_loop(0, width // block, step, 0)


def unpack_kernel(capacity, width, ids_ref, rows_ref, x_ref, prob_ref):
    first, second = one_hots(ids_ref[...], capacity)
    hot = (first + second).astype(bf16)
    block = block_of(width)

    def step(i, carry):
        cols = pl.ds(pl.multiple_of(i * block, block), block)
        x_ref[:, cols] = lax.dot_general(
            hot, rows_ref[:, cols], (((0,), (0,)), ((), ())), preferred_element_type=f32
        ).astype(bf16)
        return carry

    lax.fori_loop(0, width // block, step, 0)
    q_col = rows_ref[:, width:].astype(f32)
    prob_ref[0:1, :] = jnp.sum(first * q_col, axis=0, keepdims=True).astype(bf16)
    prob_ref[1:2, :] = jnp.sum(second * q_col, axis=0, keepdims=True).astype(bf16)


def vmem_specs(count):
    return [pl.BlockSpec(memory_space=pltpu.VMEM) for _ in range(count)]


def pack_rows(ids, probs, x, y, capacity):
    width = x.shape[1]
    return pl.pallas_call(
        lambda *refs: pack_kernel(capacity, width, *refs),
        out_shape=jax.ShapeDtypeStruct((GROUPS * capacity, 2 * width + LANES), bf16),
        in_specs=vmem_specs(4),
        out_specs=vmem_specs(1)[0],
        compiler_params=pltpu.CompilerParams(vmem_limit_bytes=40 << 20),
        name="pack_rows",
    )(ids, probs, x, y)


def unpack_rows(ids, rows, width, capacity):
    tok = ids.shape[1]
    return pl.pallas_call(
        lambda *refs: unpack_kernel(capacity, width, *refs),
        out_shape=(
            jax.ShapeDtypeStruct((tok, width), bf16),
            jax.ShapeDtypeStruct((2, tok), bf16),
        ),
        in_specs=vmem_specs(2),
        out_specs=tuple(vmem_specs(2)),
        compiler_params=pltpu.CompilerParams(vmem_limit_bytes=40 << 20),
        name="unpack_rows",
    )(ids, rows)


def term_kernel(x_ref, gate_ref, up_ref, gate_out, up_out):
    for d_ref, out in ((gate_ref, gate_out), (up_ref, up_out)):
        out[...] = lax.dot_general(
            x_ref[...], d_ref[...], (((0,), (0,)), ((), ())), preferred_element_type=f32
        ).astype(bf16)


SMALL = pl.CostEstimate(flops=1, transcendentals=0, bytes_accessed=1)


def x_terms(x_rows, gate_grad, up_grad):
    count, width = x_rows.shape
    n = gate_grad.shape[1]
    block = block_of(width)
    out = jax.ShapeDtypeStruct((width, n), bf16)
    whole = pl.BlockSpec((count, n), lambda i: (0, 0))
    part = pl.BlockSpec((block, n), lambda i: (i, 0))
    return pl.pallas_call(
        term_kernel,
        out_shape=(out, out),
        grid=(width // block,),
        in_specs=[pl.BlockSpec((count, block), lambda i: (0, i)), whole, whole],
        out_specs=(part, part),
        cost_estimate=SMALL,
        compiler_params=pltpu.CompilerParams(vmem_limit_bytes=40 << 20),
        name="x_terms",
    )(x_rows, gate_grad, up_grad)


def row_kernel(gate_ref, up_ref, w_ref, out_ref):
    half = gate_ref.shape[1]
    total = lax.dot_general(
        gate_ref[...], w_ref[:, :half], (((1,), (1,)), ((), ())), preferred_element_type=f32
    )
    total += lax.dot_general(
        up_ref[...], w_ref[:, half:], (((1,), (1,)), ((), ())), preferred_element_type=f32
    )
    out_ref[...] = total.astype(bf16)


def input_rows(gate_grad, up_grad, w_gate_up):
    count, n = gate_grad.shape
    width = w_gate_up.shape[0]
    block = block_of(width)
    whole = pl.BlockSpec((count, n), lambda i: (0, 0))
    return pl.pallas_call(
        row_kernel,
        out_shape=jax.ShapeDtypeStruct((count, width), bf16),
        grid=(width // block,),
        in_specs=[whole, whole, pl.BlockSpec((block, 2 * n), lambda i: (i, 0))],
        out_specs=pl.BlockSpec((count, block), lambda i: (0, i)),
        cost_estimate=SMALL,
        compiler_params=pltpu.CompilerParams(vmem_limit_bytes=40 << 20),
        name="input_rows",
    )(gate_grad, up_grad, w_gate_up)


def put_kernel(count, rows_ref, *refs):
    pieces, out_ref, sems = refs[:count], refs[-2], refs[-1]
    copies = [
        pltpu.make_async_copy(
            piece,
            out_ref.at[pl.ds(pl.multiple_of(rows_ref[i], 16), piece.shape[0])],
            sems.at[i],
        )
        for i, piece in enumerate(pieces)
    ]
    for copy in copies:
        copy.start()
    for copy in copies:
        copy.wait()


def put(whole, height, placed):
    pieces = [piece for piece, _ in placed]
    count = len(pieces)
    starts = jnp.stack([row for _, row in placed]).astype(jnp.int32)
    old = [] if whole is None else [whole]
    out = jax.ShapeDtypeStruct((height, pieces[0].shape[1]), bf16)
    moved = sum(piece.size for piece in pieces) * 4
    return pl.pallas_call(
        lambda *refs: put_kernel(count, *refs),
        out_shape=out,
        in_specs=[pl.BlockSpec(memory_space=pltpu.SMEM)]
        + [pl.BlockSpec(memory_space=pl.ANY) for _ in pieces + old],
        out_specs=pl.BlockSpec(memory_space=pl.ANY),
        scratch_shapes=[pltpu.SemaphoreType.DMA((count,))],
        input_output_aliases={1 + count: 0} if old else {},
        cost_estimate=pl.CostEstimate(flops=0, transcendentals=0, bytes_accessed=moved),
        name="put_rows",
    )(starts, *pieces, *old)


def neighbours(part):
    return lax.ppermute(part, "x", PLUS), lax.ppermute(part, "x", MINUS)


def far(left, right, half):
    return lax.ppermute(left[:half], "x", PLUS), lax.ppermute(right[half:], "x", MINUS)


def plus(*values):
    return sum(v.astype(f32) for v in values).astype(bf16)


def send(pair):
    to_right, to_left = pair
    return lax.ppermute(to_right, "x", PLUS), lax.ppermute(to_left, "x", MINUS)


class Scatter:
    def __init__(self, terms, x, yh):
        self.terms, self.x, self.yh = terms, x, yh
        self.size, self.n = terms.shape[0] // 8, terms.shape[1]

    def rows(self, k, side, count):
        start = self.size * (2 * ((self.x + k) % 4) + side)
        return lax.dynamic_slice(self.terms, (start, 0), (count * self.size, self.n))

    def first(self):
        to_right = jnp.concatenate((self.rows(2, 0, 1), self.rows(1, 1, 1)))
        to_left = jnp.concatenate((self.rows(2, 1, 1), self.rows(3, 0, 1)))
        return to_right, to_left

    def second(self, got):
        from_left, from_right = got
        self.low, self.top = from_left[self.size :], from_right[self.size :]
        to_right = plus(self.rows(1, 0, 1), from_left[: self.size])
        to_left = plus(self.rows(3, 1, 1), from_right[: self.size])
        return to_right, to_left

    def mine(self, side):
        top, low = self.got
        return plus(
            self.rows(0, side, 1),
            jnp.where(side == 0, top, self.low),
            jnp.where(side == 0, self.top, low),
        )

    def third(self):
        self.kept = self.mine(self.yh)
        return lax.ppermute(self.mine(1 - self.yh), "yh", SWAP)

    def last(self, sent):
        return plus(self.kept, sent)


def body(
    layer_input,
    output_grad,
    expert_ids,
    gate_probs,
    gate_weight,
    up_weight,
    down_weight,
    gate_moment,
    up_moment,
    down_moment,
    gate_second,
    up_second,
    down_second,
):
    x, yh, yl = lax.axis_index("x"), lax.axis_index("yh"), lax.axis_index("yl")
    z, c = lax.axis_index("z"), lax.axis_index("c")
    tok, picks = expert_ids.shape
    capacity = 3 * tok * picks // (2 * GROUPS)
    width = layer_input.shape[1]
    hidden_units = gate_weight.shape[2]
    quarter = hidden_units // 4
    half = hidden_units // 2
    rows = GROUPS * capacity
    depth = gate_weight.shape[1]

    gate_low, up_low = gate_weight[0].astype(bf16), up_weight[0].astype(bf16)

    def chunk(core):
        cuts = [
            w[:, (core + 2 * k) * quarter : (core + 2 * k + 1) * quarter]
            for w in (gate_low, up_low)
            for k in range(2)
        ]
        return jnp.concatenate(cuts, axis=1)

    chunks = (chunk(0), chunk(1))
    part_a = lax.ppermute(jnp.where(yl == 0, chunks[0], chunks[1]), ("yl", "c"), PAIR_A)
    part_b = lax.ppermute(jnp.where(yl == 0, chunks[1], chunks[0]), ("yl", "c"), PAIR_B)
    down_part = lax.ppermute(down_weight[0].astype(bf16), CYCLE_AXES, CYCLE)
    part_a, part_b, down_part = join((part_a, part_b, down_part))
    part = jnp.where(
        c == 0, jnp.concatenate((part_a, part_b)), jnp.concatenate((part_b, part_a))
    )

    part_other = lax.ppermute(part, "yh", SWAP)
    down_other = lax.ppermute(down_part, "yh", SWAP)
    near_own = join(neighbours(part))
    far_own = far(*near_own, depth)
    part_other, down_other, far_own = join((part_other, down_other, far_own))

    size_down = down_part.shape[0]
    both = jnp.where(
        yh == 0,
        jnp.concatenate((down_part, down_other)),
        jnp.concatenate((down_other, down_part)),
    )

    def gate_up_row(k, side):
        return 2 * depth * (2 * ((x + k) % 4) + side)

    def down_row(k):
        return 2 * size_down * ((x + k) % 4)

    def ring_rows(row, part, left, right):
        return [(part, row(0)), (left, row(3)), (right, row(1))]

    def far_rows_of(row, top, low):
        return [(top, row(2)), (low, row(2) + top.shape[0])]

    own_row = lambda k: gate_up_row(k, yh)
    other_row = lambda k: gate_up_row(k, 1 - yh)
    ids = expert_ids.T
    sent = pack_rows(ids, gate_probs.T.astype(f32), layer_input, output_grad, capacity)
    sent, both, part_other, near_own, far_own = join((sent, both, part_other, near_own, far_own))
    near_other = neighbours(part_other)
    own = lax.all_to_all(
        sent.reshape(GROUPS, capacity, -1), ("yl", "z"), 0, 0, tiled=True
    ).reshape(rows, -1)
    w_gate_up = put(
        None,
        width,
        ring_rows(own_row, part, *near_own) + far_rows_of(own_row, *far_own),
    )
    near_other, w_gate_up, both = join((near_other, w_gate_up, both))
    near_down = neighbours(both)
    far_other = far(*near_other, depth)
    w_gate_up = put(w_gate_up, width, ring_rows(other_row, part_other, *near_other))
    own, near_down, far_other, w_gate_up = join((own, near_down, far_other, w_gate_up))
    far_down = far(*near_down, size_down)
    w_gate_up = put(w_gate_up, width, far_rows_of(other_row, *far_other))
    w_down = put(None, half, ring_rows(down_row, both, *near_down))
    other = lax.ppermute(own, "c", SWAP)
    x_rows = jnp.concatenate((own[:, :width], other[:, :width]))
    y_rows = jnp.concatenate((own[:, width : 2 * width], other[:, width : 2 * width]))
    gates = jnp.concatenate((own[:, 2 * width :], other[:, 2 * width :]))[:, :1].astype(f32)

    pre = jnp.dot(x_rows, w_gate_up, preferred_element_type=f32)
    gate_pre, up_pre = pre[:, :half], pre[:, half:]
    sigmoid_gate = jax.nn.sigmoid(gate_pre)
    silu_gate = gate_pre * sigmoid_gate
    hidden_full = silu_gate * up_pre
    hidden = hidden_full.astype(bf16)
    hidden_scaled = (gates * hidden_full).astype(bf16)
    down_term = lax.dot_general(
        hidden_scaled, y_rows, (((0,), (0,)), ((), ())), preferred_element_type=f32
    ).astype(bf16)
    down_sum = Scatter(down_term, x, yh)
    down_send = down_sum.first()
    far_down, down_send = join((far_down, down_send))
    w_down = put(w_down, half, far_rows_of(down_row, *far_down))
    down_got = send(down_send)
    raw_grad = lax.dot_general(
        y_rows, w_down, (((1,), (1,)), ((), ())), preferred_element_type=f32
    )
    prob_rows = jnp.sum(hidden.astype(f32) * raw_grad, axis=1, keepdims=True)
    hidden_grad = gates * raw_grad
    dsilu = sigmoid_gate * (1.0 + gate_pre * (1.0 - sigmoid_gate))
    gate_grad = (hidden_grad * up_pre * dsilu).astype(bf16)
    up_grad = (hidden_grad * silu_gate).astype(bf16)

    gate_term, up_term = x_terms(x_rows, gate_grad, up_grad)
    gate_sum, up_sum = Scatter(gate_term, x, yh), Scatter(up_term, x, yh)

    down_got, gate_sum.terms, up_sum.terms = join((down_got, gate_sum.terms, up_sum.terms))
    down_send = down_sum.second(down_got)
    gate_send = gate_sum.first()
    gate_grad, up_grad, down_send, gate_send = join(
        (gate_grad, up_grad, down_send, gate_send)
    )
    down_got, gate_got = send(down_send), send(gate_send)
    far_part = input_rows(gate_grad[rows:], up_grad[rows:], w_gate_up)
    far_rows = lax.ppermute(far_part, "c", SWAP)
    far_prob = jnp.broadcast_to(prob_rows[rows:], (rows, LANES))
    far_prob = lax.ppermute(far_prob, "c", SWAP)
    near_rows = (
        input_rows(gate_grad[:rows], up_grad[:rows], w_gate_up).astype(f32)
        + far_rows.astype(f32)
    ).astype(bf16)
    near_prob = (prob_rows[:rows] + far_prob).astype(bf16)
    packed = jnp.concatenate((near_rows, near_prob), axis=1)
    packed, gate_got, down_sum.got = join((packed, gate_got, down_got))
    gate_send, up_send = join((gate_sum.second(gate_got), up_sum.first()))
    gate_got, up_got = send(gate_send), send(up_send)
    down_sent = down_sum.third()
    up_got, gate_sum.got, down_sent = join((up_got, gate_got, down_sent))
    returned = lax.all_to_all(
        packed.reshape(GROUPS, capacity, -1), ("yl", "z"), 0, 0, tiled=True
    ).reshape(rows, -1)
    def send_home(grad):
        return tuple(
            lax.ppermute(
                lax.dynamic_slice(grad, (depth * start, 0), (depth, half)),
                ("yl", "c"),
                back(pairs),
            )
            for start, pairs in ((c, PAIR_A), (1 - c, PAIR_B))
        )

    def natural(home):
        even = jnp.where(yl == 0, home[0], home[1])
        odd = jnp.where(yl == 0, home[1], home[0])
        return jnp.concatenate(
            [v[:, k * quarter : (k + 1) * quarter] for k in range(2) for v in (even, odd)],
            axis=1,
        )[None].astype(f32)

    down_home = down_sum.last(down_sent)
    up_send, gate_sum.got, down_home = join((up_sum.second(up_got), gate_sum.got, down_home))
    up_got = send(up_send)
    gate_sent = gate_sum.third()
    down_home = lax.ppermute(down_home, CYCLE_AXES, back(CYCLE))
    up_sum.got, gate_sent, down_home, returned = join((up_got, gate_sent, down_home, returned))
    up_mine, gate_sent = join((up_sum.mine(1 - yh), gate_sent))
    up_sent = lax.ppermute(up_mine, "yh", SWAP)
    up_sum.kept = up_sum.mine(yh)
    gate_home = send_home(gate_sum.last(gate_sent))
    new_down_weight, new_down_moment, new_down_second = adamw(
        down_weight, down_moment, down_second, down_home.astype(f32)[None]
    )
    up_sent, gate_home = join((up_sent, gate_home))
    up_home = send_home(up_sum.last(up_sent))
    input_grad, prob_grad = unpack_rows(ids, returned, width, capacity)
    new_gate_weight, new_gate_moment, new_gate_second = adamw(
        gate_weight, gate_moment, gate_second, natural(gate_home)
    )
    up_home, new_gate_weight = join((up_home, new_gate_weight))
    new_up_weight, new_up_moment, new_up_second = adamw(
        up_weight, up_moment, up_second, natural(up_home)
    )
    return (
        input_grad,
        prob_grad.T,
        new_gate_weight,
        new_up_weight,
        new_down_weight,
        new_gate_moment,
        new_up_moment,
        new_down_moment,
        new_gate_second,
        new_up_second,
        new_down_second,
    )


def solution(mesh):
    fine = Mesh(mesh.devices.reshape(4, 2, 2, 4, 2), ("x", "yh", "yl", "z", "c"))
    tokens = P(("x", "yh", "yl", "z", "c"), None)
    weights = P(("z", "c"), ("x", "yh", "yl"), None)
    return jax.shard_map(
        body,
        mesh=fine,
        in_specs=(tokens,) * 4 + (weights,) * 9,
        out_specs=(tokens,) * 2 + (weights,) * 9,
        check_vma=False,
    )
```

```python
import jax
import jax.numpy as jnp
from jax import lax
from jax.experimental import pallas as pl
from jax.experimental.pallas import tpu as pltpu
from jax.sharding import Mesh
from jax.sharding import PartitionSpec as P

beta_one = 0.9
beta_two = 0.95
learn_rate = 0.003
decay_rate = 0.1
epsilon = 1e-08
correct_one = 1.0 - 2.6561398887587e-05
correct_two = 1.0 - 0.005920529220333

LANES = 128
GROUPS = 8
f32 = jnp.float32
bf16 = jnp.bfloat16

PLUS = [(i, (i + 1) % 4) for i in range(4)]
MINUS = [(i, (i - 1) % 4) for i in range(4)]
SWAP = [(0, 1), (1, 0)]
PAIR_A = [(2 * yl + c, 2 * c + yl) for yl in range(2) for c in range(2)]
PAIR_B = [(2 * yl + c, 2 * c + 1 - yl) for yl in range(2) for c in range(2)]


def _cycle():
    pairs = []
    for x1 in range(2):
        for x0 in range(2):
            for yh in range(2):
                for yl in range(2):
                    for c in range(2):
                        src = (((x1 * 2 + x0) * 2 + yh) * 2 + yl) * 2 + c
                        dst = (((x1 * 2 + yh) * 2 + yl) * 2 + c) * 2 + x0
                        pairs.append((src, dst))
    return pairs


CYCLE = _cycle()
CYCLE_AXES = ("x", "yh", "yl", "c")


def back(pairs):
    return [(d, s) for s, d in pairs]


join = lax.optimization_barrier


def adamw(weight, moment, second, grad):
    moment_new = beta_one * moment + (1.0 - beta_one) * grad
    second_new = beta_two * second + (1.0 - beta_two) * grad * grad
    update = moment_new / correct_one / (jnp.sqrt(second_new / correct_two) + epsilon)
    return (weight - learn_rate * (update + decay_rate * weight), moment_new, second_new)


def one_hots(ids, capacity):
    tok = ids.shape[1]
    experts = lax.broadcasted_iota(jnp.int32, (GROUPS, tok), 0)
    named = [(experts == ids[k : k + 1, :]).astype(f32) for k in range(2)]
    earlier = (
        lax.broadcasted_iota(jnp.int32, (tok, tok), 0)
        < lax.broadcasted_iota(jnp.int32, (tok, tok), 1)
    ).astype(f32)
    count = jnp.dot(
        (named[0] + named[1]).astype(bf16), earlier.astype(bf16), preferred_element_type=f32
    )
    slot = lax.broadcasted_iota(jnp.int32, (GROUPS * capacity, tok), 0)
    hots = []
    for k in range(2):
        rank = jnp.sum(named[k] * count, axis=0, keepdims=True).astype(jnp.int32)
        expert = ids[k : k + 1, :]
        dest = ((expert & 1) * 4 + (expert >> 1)) * capacity + rank
        hots.append((slot == dest).astype(f32))
    return hots


def block_of(width):
    return 512 if width % 512 == 0 else width


def pack_kernel(capacity, width, ids_ref, probs_ref, x_ref, y_ref, out_ref):
    first, second = one_hots(ids_ref[...], capacity)
    hot = (first + second).astype(bf16)
    probs = probs_ref[...]
    gates = (first * probs[0:1, :] + second * probs[1:2, :]).astype(bf16)
    ones = jnp.ones((gates.shape[1], LANES), bf16)
    out_ref[:, 2 * width :] = jnp.dot(gates, ones, preferred_element_type=f32).astype(bf16)
    block = block_of(width)

    def step(i, carry):
        at = pl.multiple_of(i * block, block)
        cols = pl.ds(at, block)
        out_ref[:, cols] = jnp.dot(
            hot, x_ref[:, cols], preferred_element_type=f32
        ).astype(bf16)
        out_ref[:, pl.ds(pl.multiple_of(at + width, block), block)] = jnp.dot(
            hot, y_ref[:, cols], preferred_element_type=f32
        ).astype(bf16)
        return carry

    lax.fori_loop(0, width // block, step, 0)


def unpack_kernel(capacity, width, ids_ref, rows_ref, x_ref, prob_ref):
    first, second = one_hots(ids_ref[...], capacity)
    hot = (first + second).astype(bf16)
    block = block_of(width)

    def step(i, carry):
        cols = pl.ds(pl.multiple_of(i * block, block), block)
        x_ref[:, cols] = lax.dot_general(
            hot, rows_ref[:, cols], (((0,), (0,)), ((), ())), preferred_element_type=f32
        ).astype(bf16)
        return carry

    lax.fori_loop(0, width // block, step, 0)
    q_col = rows_ref[:, width:].astype(f32)
    prob_ref[0:1, :] = jnp.sum(first * q_col, axis=0, keepdims=True).astype(bf16)
    prob_ref[1:2, :] = jnp.sum(second * q_col, axis=0, keepdims=True).astype(bf16)


def vmem_specs(count):
    return [pl.BlockSpec(memory_space=pltpu.VMEM) for _ in range(count)]


def pack_rows(ids, probs, x, y, capacity):
    width = x.shape[1]
    return pl.pallas_call(
        lambda *refs: pack_kernel(capacity, width, *refs),
        out_shape=jax.ShapeDtypeStruct((GROUPS * capacity, 2 * width + LANES), bf16),
        in_specs=vmem_specs(4),
        out_specs=vmem_specs(1)[0],
        compiler_params=pltpu.CompilerParams(vmem_limit_bytes=40 << 20),
        name="pack_rows",
    )(ids, probs, x, y)


def unpack_rows(ids, rows, width, capacity):
    tok = ids.shape[1]
    return pl.pallas_call(
        lambda *refs: unpack_kernel(capacity, width, *refs),
        out_shape=(
            jax.ShapeDtypeStruct((tok, width), bf16),
            jax.ShapeDtypeStruct((2, tok), bf16),
        ),
        in_specs=vmem_specs(2),
        out_specs=tuple(vmem_specs(2)),
        compiler_params=pltpu.CompilerParams(vmem_limit_bytes=40 << 20),
        name="unpack_rows",
    )(ids, rows)


def term_kernel(x_ref, gate_ref, up_ref, gate_out, up_out):
    for d_ref, out in ((gate_ref, gate_out), (up_ref, up_out)):
        out[...] = lax.dot_general(
            x_ref[...], d_ref[...], (((0,), (0,)), ((), ())), preferred_element_type=f32
        ).astype(bf16)


SMALL = pl.CostEstimate(flops=1, transcendentals=0, bytes_accessed=1)


def x_terms(x_rows, gate_grad, up_grad):
    count, width = x_rows.shape
    n = gate_grad.shape[1]
    block = block_of(width)
    out = jax.ShapeDtypeStruct((width, n), bf16)
    whole = pl.BlockSpec((count, n), lambda i: (0, 0))
    part = pl.BlockSpec((block, n), lambda i: (i, 0))
    return pl.pallas_call(
        term_kernel,
        out_shape=(out, out),
        grid=(width // block,),
        in_specs=[pl.BlockSpec((count, block), lambda i: (0, i)), whole, whole],
        out_specs=(part, part),
        cost_estimate=SMALL,
        compiler_params=pltpu.CompilerParams(vmem_limit_bytes=40 << 20),
        name="x_terms",
    )(x_rows, gate_grad, up_grad)


def row_kernel(gate_ref, up_ref, w_ref, out_ref):
    half = gate_ref.shape[1]
    total = lax.dot_general(
        gate_ref[...], w_ref[:, :half], (((1,), (1,)), ((), ())), preferred_element_type=f32
    )
    total += lax.dot_general(
        up_ref[...], w_ref[:, half:], (((1,), (1,)), ((), ())), preferred_element_type=f32
    )
    out_ref[...] = total.astype(bf16)


def input_rows(gate_grad, up_grad, w_gate_up):
    count, n = gate_grad.shape
    width = w_gate_up.shape[0]
    block = block_of(width)
    whole = pl.BlockSpec((count, n), lambda i: (0, 0))
    return pl.pallas_call(
        row_kernel,
        out_shape=jax.ShapeDtypeStruct((count, width), bf16),
        grid=(width // block,),
        in_specs=[whole, whole, pl.BlockSpec((block, 2 * n), lambda i: (i, 0))],
        out_specs=pl.BlockSpec((count, block), lambda i: (0, i)),
        cost_estimate=SMALL,
        compiler_params=pltpu.CompilerParams(vmem_limit_bytes=40 << 20),
        name="input_rows",
    )(gate_grad, up_grad, w_gate_up)


def put_kernel(count, rows_ref, *refs):
    pieces, out_ref, sems = refs[:count], refs[-2], refs[-1]
    copies = [
        pltpu.make_async_copy(
            piece,
            out_ref.at[pl.ds(pl.multiple_of(rows_ref[i], 16), piece.shape[0])],
            sems.at[i],
        )
        for i, piece in enumerate(pieces)
    ]
    for copy in copies:
        copy.start()
    for copy in copies:
        copy.wait()


def put(whole, height, placed):
    pieces = [piece for piece, _ in placed]
    count = len(pieces)
    starts = jnp.stack([row for _, row in placed]).astype(jnp.int32)
    old = [] if whole is None else [whole]
    out = jax.ShapeDtypeStruct((height, pieces[0].shape[1]), bf16)
    moved = sum(piece.size for piece in pieces) * 4
    return pl.pallas_call(
        lambda *refs: put_kernel(count, *refs),
        out_shape=out,
        in_specs=[pl.BlockSpec(memory_space=pltpu.SMEM)]
        + vmem_specs(count)
        + [pl.BlockSpec(memory_space=pl.ANY) for _ in old],
        out_specs=pl.BlockSpec(memory_space=pl.ANY),
        scratch_shapes=[pltpu.SemaphoreType.DMA((count,))],
        input_output_aliases={1 + count: 0} if old else {},
        cost_estimate=pl.CostEstimate(flops=0, transcendentals=0, bytes_accessed=moved),
        compiler_params=pltpu.CompilerParams(vmem_limit_bytes=40 << 20),
        name="put_rows",
    )(starts, *pieces, *old)


def neighbours(part):
    return lax.ppermute(part, "x", PLUS), lax.ppermute(part, "x", MINUS)


def far(left, right, half):
    return lax.ppermute(left[:half], "x", PLUS), lax.ppermute(right[half:], "x", MINUS)


def plus(*values):
    return sum(v.astype(f32) for v in values).astype(bf16)


def send(pair):
    to_right, to_left = pair
    return lax.ppermute(to_right, "x", PLUS), lax.ppermute(to_left, "x", MINUS)


class Scatter:
    def __init__(self, terms, x, yh):
        self.terms, self.x, self.yh = terms, x, yh
        self.size, self.n = terms.shape[0] // 8, terms.shape[1]

    def rows(self, k, side, count):
        start = self.size * (2 * ((self.x + k) % 4) + side)
        return lax.dynamic_slice(self.terms, (start, 0), (count * self.size, self.n))

    def first(self):
        to_right = jnp.concatenate((self.rows(2, 0, 1), self.rows(1, 1, 1)))
        to_left = jnp.concatenate((self.rows(2, 1, 1), self.rows(3, 0, 1)))
        return to_right, to_left

    def second(self, got):
        from_left, from_right = got
        self.low, self.top = from_left[self.size :], from_right[self.size :]
        to_right = plus(self.rows(1, 0, 1), from_left[: self.size])
        to_left = plus(self.rows(3, 1, 1), from_right[: self.size])
        return to_right, to_left

    def mine(self, side):
        top, low = self.got
        return plus(
            self.rows(0, side, 1),
            jnp.where(side == 0, top, self.low),
            jnp.where(side == 0, self.top, low),
        )

    def third(self):
        self.kept = self.mine(self.yh)
        return lax.ppermute(self.mine(1 - self.yh), "yh", SWAP)

    def last(self, sent):
        return plus(self.kept, sent)


def body(
    layer_input,
    output_grad,
    expert_ids,
    gate_probs,
    gate_weight,
    up_weight,
    down_weight,
    gate_moment,
    up_moment,
    down_moment,
    gate_second,
    up_second,
    down_second,
):
    x, yh, yl = lax.axis_index("x"), lax.axis_index("yh"), lax.axis_index("yl")
    z, c = lax.axis_index("z"), lax.axis_index("c")
    tok, picks = expert_ids.shape
    capacity = 3 * tok * picks // (2 * GROUPS)
    width = layer_input.shape[1]
    hidden_units = gate_weight.shape[2]
    quarter = hidden_units // 4
    half = hidden_units // 2
    rows = GROUPS * capacity
    depth = gate_weight.shape[1]

    gate_low, up_low = gate_weight[0].astype(bf16), up_weight[0].astype(bf16)

    def chunk(core):
        cuts = [
            w[:, (core + 2 * k) * quarter : (core + 2 * k + 1) * quarter]
            for w in (gate_low, up_low)
            for k in range(2)
        ]
        return jnp.concatenate(cuts, axis=1)

    chunks = (chunk(0), chunk(1))
    part_a = lax.ppermute(jnp.where(yl == 0, chunks[0], chunks[1]), ("yl", "c"), PAIR_A)
    part_b = lax.ppermute(jnp.where(yl == 0, chunks[1], chunks[0]), ("yl", "c"), PAIR_B)
    down_part = lax.ppermute(down_weight[0].astype(bf16), CYCLE_AXES, CYCLE)
    part_a, part_b, down_part = join((part_a, part_b, down_part))
    part = jnp.where(
        c == 0, jnp.concatenate((part_a, part_b)), jnp.concatenate((part_b, part_a))
    )

    part_other = lax.ppermute(part, "yh", SWAP)
    down_other = lax.ppermute(down_part, "yh", SWAP)
    near_own = join(neighbours(part))
    far_own = far(*near_own, depth)
    part_other, down_other, far_own = join((part_other, down_other, far_own))

    size_down = down_part.shape[0]
    both = jnp.where(
        yh == 0,
        jnp.concatenate((down_part, down_other)),
        jnp.concatenate((down_other, down_part)),
    )

    def gate_up_row(k, side):
        return 2 * depth * (2 * ((x + k) % 4) + side)

    def down_row(k):
        return 2 * size_down * ((x + k) % 4)

    def ring_rows(row, part, left, right):
        return [(part, row(0)), (left, row(3)), (right, row(1))]

    def far_rows_of(row, top, low):
        return [(top, row(2)), (low, row(2) + top.shape[0])]

    own_row = lambda k: gate_up_row(k, yh)
    other_row = lambda k: gate_up_row(k, 1 - yh)
    ids = expert_ids.T
    sent = pack_rows(ids, gate_probs.T.astype(f32), layer_input, output_grad, capacity)
    sent, both, part_other, near_own, far_own = join((sent, both, part_other, near_own, far_own))
    near_other = neighbours(part_other)
    own = lax.all_to_all(
        sent.reshape(GROUPS, capacity, -1), ("yl", "z"), 0, 0, tiled=True
    ).reshape(rows, -1)
    w_gate_up = put(
        None,
        width,
        ring_rows(own_row, part, *near_own) + far_rows_of(own_row, *far_own),
    )
    near_other, w_gate_up, both = join((near_other, w_gate_up, both))
    near_down = neighbours(both)
    far_other = far(*near_other, depth)
    w_gate_up = put(w_gate_up, width, ring_rows(other_row, part_other, *near_other))
    own, near_down, far_other, w_gate_up = join((own, near_down, far_other, w_gate_up))
    far_down = far(*near_down, size_down)
    w_gate_up = put(w_gate_up, width, far_rows_of(other_row, *far_other))
    w_down = put(None, half, ring_rows(down_row, both, *near_down))
    other = lax.ppermute(own, "c", SWAP)
    x_rows = jnp.concatenate((own[:, :width], other[:, :width]))
    y_rows = jnp.concatenate((own[:, width : 2 * width], other[:, width : 2 * width]))
    gates = jnp.concatenate((own[:, 2 * width :], other[:, 2 * width :]))[:, :1].astype(f32)

    pre = jnp.dot(x_rows, w_gate_up, preferred_element_type=f32)
    gate_pre, up_pre = pre[:, :half], pre[:, half:]
    sigmoid_gate = jax.nn.sigmoid(gate_pre)
    silu_gate = gate_pre * sigmoid_gate
    hidden_full = silu_gate * up_pre
    hidden = hidden_full.astype(bf16)
    hidden_scaled = (gates * hidden_full).astype(bf16)
    down_term = lax.dot_general(
        hidden_scaled, y_rows, (((0,), (0,)), ((), ())), preferred_element_type=f32
    ).astype(bf16)
    down_sum = Scatter(down_term, x, yh)
    down_send = down_sum.first()
    far_down, down_send = join((far_down, down_send))
    w_down = put(w_down, half, far_rows_of(down_row, *far_down))
    down_got = send(down_send)
    raw_grad = lax.dot_general(
        y_rows, w_down, (((1,), (1,)), ((), ())), preferred_element_type=f32
    )
    prob_rows = jnp.sum(hidden.astype(f32) * raw_grad, axis=1, keepdims=True)
    hidden_grad = gates * raw_grad
    dsilu = sigmoid_gate * (1.0 + gate_pre * (1.0 - sigmoid_gate))
    gate_grad = (hidden_grad * up_pre * dsilu).astype(bf16)
    up_grad = (hidden_grad * silu_gate).astype(bf16)

    gate_term, up_term = x_terms(x_rows, gate_grad, up_grad)
    gate_sum, up_sum = Scatter(gate_term, x, yh), Scatter(up_term, x, yh)

    far_part = input_rows(gate_grad[rows:], up_grad[rows:], w_gate_up)
    far_prob = jnp.broadcast_to(prob_rows[rows:], (rows, LANES))
    far_prob = lax.ppermute(far_prob, "c", SWAP)
    gate_send = gate_sum.first()
    down_got, gate_send, far_part, far_prob = join((down_got, gate_send, far_part, far_prob))
    down_send = down_sum.second(down_got)
    gate_grad, up_grad, down_send, gate_send = join(
        (gate_grad, up_grad, down_send, gate_send)
    )
    down_got, gate_got = send(down_send), send(gate_send)
    far_rows = lax.ppermute(far_part, "c", SWAP)
    near_rows = (
        input_rows(gate_grad[:rows], up_grad[:rows], w_gate_up).astype(f32)
        + far_rows.astype(f32)
    ).astype(bf16)
    near_prob = (prob_rows[:rows] + far_prob).astype(bf16)
    packed = jnp.concatenate((near_rows, near_prob), axis=1)
    packed, gate_got, down_sum.got = join((packed, gate_got, down_got))
    gate_send, up_send = join((gate_sum.second(gate_got), up_sum.first()))
    gate_got, up_got = send(gate_send), send(up_send)
    down_sent = down_sum.third()
    up_got, gate_sum.got, down_sent = join((up_got, gate_got, down_sent))
    returned = lax.all_to_all(
        packed.reshape(GROUPS, capacity, -1), ("yl", "z"), 0, 0, tiled=True
    ).reshape(rows, -1)
    def send_home(grad):
        return tuple(
            lax.ppermute(
                lax.dynamic_slice(grad, (depth * start, 0), (depth, half)),
                ("yl", "c"),
                back(pairs),
            )
            for start, pairs in ((c, PAIR_A), (1 - c, PAIR_B))
        )

    def natural(home):
        even = jnp.where(yl == 0, home[0], home[1])
        odd = jnp.where(yl == 0, home[1], home[0])
        return jnp.concatenate(
            [v[:, k * quarter : (k + 1) * quarter] for k in range(2) for v in (even, odd)],
            axis=1,
        )[None].astype(f32)

    down_home = down_sum.last(down_sent)
    up_send, gate_sum.got, down_home = join((up_sum.second(up_got), gate_sum.got, down_home))
    up_got = send(up_send)
    gate_sent = gate_sum.third()
    down_home = lax.ppermute(down_home, CYCLE_AXES, back(CYCLE))
    up_sum.got, gate_sent, down_home, returned = join((up_got, gate_sent, down_home, returned))
    up_mine, gate_sent = join((up_sum.mine(1 - yh), gate_sent))
    up_sent = lax.ppermute(up_mine, "yh", SWAP)
    up_sum.kept = up_sum.mine(yh)
    gate_home = send_home(gate_sum.last(gate_sent))
    new_down_weight, new_down_moment, new_down_second = adamw(
        down_weight, down_moment, down_second, down_home.astype(f32)[None]
    )
    up_sent, gate_home = join((up_sent, gate_home))
    up_home = send_home(up_sum.last(up_sent))
    input_grad, prob_grad = unpack_rows(ids, returned, width, capacity)
    new_gate_weight, new_gate_moment, new_gate_second = adamw(
        gate_weight, gate_moment, gate_second, natural(gate_home)
    )
    up_home, new_gate_weight = join((up_home, new_gate_weight))
    new_up_weight, new_up_moment, new_up_second = adamw(
        up_weight, up_moment, up_second, natural(up_home)
    )
    return (
        input_grad,
        prob_grad.T,
        new_gate_weight,
        new_up_weight,
        new_down_weight,
        new_gate_moment,
        new_up_moment,
        new_down_moment,
        new_gate_second,
        new_up_second,
        new_down_second,
    )


def solution(mesh):
    fine = Mesh(mesh.devices.reshape(4, 2, 2, 4, 2), ("x", "yh", "yl", "z", "c"))
    tokens = P(("x", "yh", "yl", "z", "c"), None)
    weights = P(("z", "c"), ("x", "yh", "yl"), None)
    return jax.shard_map(
        body,
        mesh=fine,
        in_specs=(tokens,) * 4 + (weights,) * 9,
        out_specs=(tokens,) * 2 + (weights,) * 9,
        check_vma=False,
    )
```

```python
import jax
import jax.numpy as jnp
from jax import lax
from jax.experimental import pallas as pl
from jax.experimental.pallas import tpu as pltpu
from jax.sharding import Mesh
from jax.sharding import PartitionSpec as P

beta_one = 0.9
beta_two = 0.95
learn_rate = 0.003
decay_rate = 0.1
epsilon = 1e-08
correct_one = 1.0 - 2.6561398887587e-05
correct_two = 1.0 - 0.005920529220333

LANES = 128
GROUPS = 8
f32 = jnp.float32
bf16 = jnp.bfloat16

PLUS = [(i, (i + 1) % 4) for i in range(4)]
MINUS = [(i, (i - 1) % 4) for i in range(4)]
SWAP = [(0, 1), (1, 0)]
PAIR_A = [(2 * yl + c, 2 * c + yl) for yl in range(2) for c in range(2)]
PAIR_B = [(2 * yl + c, 2 * c + 1 - yl) for yl in range(2) for c in range(2)]


def _cycle():
    pairs = []
    for x1 in range(2):
        for x0 in range(2):
            for yh in range(2):
                for yl in range(2):
                    for c in range(2):
                        src = (((x1 * 2 + x0) * 2 + yh) * 2 + yl) * 2 + c
                        dst = (((x1 * 2 + yh) * 2 + yl) * 2 + c) * 2 + x0
                        pairs.append((src, dst))
    return pairs


CYCLE = _cycle()
CYCLE_AXES = ("x", "yh", "yl", "c")


def back(pairs):
    return [(d, s) for s, d in pairs]


join = lax.optimization_barrier


def adamw(weight, moment, second, grad):
    moment_new = beta_one * moment + (1.0 - beta_one) * grad
    second_new = beta_two * second + (1.0 - beta_two) * grad * grad
    update = moment_new / correct_one / (jnp.sqrt(second_new / correct_two) + epsilon)
    return (weight - learn_rate * (update + decay_rate * weight), moment_new, second_new)


def one_hots(ids, capacity):
    tok = ids.shape[1]
    experts = lax.broadcasted_iota(jnp.int32, (GROUPS, tok), 0)
    named = [(experts == ids[k : k + 1, :]).astype(f32) for k in range(2)]
    earlier = (
        lax.broadcasted_iota(jnp.int32, (tok, tok), 0)
        < lax.broadcasted_iota(jnp.int32, (tok, tok), 1)
    ).astype(f32)
    count = jnp.dot(
        (named[0] + named[1]).astype(bf16), earlier.astype(bf16), preferred_element_type=f32
    )
    slot = lax.broadcasted_iota(jnp.int32, (GROUPS * capacity, tok), 0)
    hots = []
    for k in range(2):
        rank = jnp.sum(named[k] * count, axis=0, keepdims=True).astype(jnp.int32)
        expert = ids[k : k + 1, :]
        dest = ((expert & 1) * 4 + (expert >> 1)) * capacity + rank
        hots.append((slot == dest).astype(f32))
    return hots


def block_of(width):
    return 512 if width % 512 == 0 else width


def pack_kernel(capacity, width, ids_ref, probs_ref, x_ref, y_ref, out_ref):
    first, second = one_hots(ids_ref[...], capacity)
    hot = (first + second).astype(bf16)
    probs = probs_ref[...]
    gates = (first * probs[0:1, :] + second * probs[1:2, :]).astype(bf16)
    ones = jnp.ones((gates.shape[1], LANES), bf16)
    out_ref[:, 2 * width :] = jnp.dot(gates, ones, preferred_element_type=f32).astype(bf16)
    block = block_of(width)

    def step(i, carry):
        at = pl.multiple_of(i * block, block)
        cols = pl.ds(at, block)
        out_ref[:, cols] = jnp.dot(
            hot, x_ref[:, cols], preferred_element_type=f32
        ).astype(bf16)
        out_ref[:, pl.ds(pl.multiple_of(at + width, block), block)] = jnp.dot(
            hot, y_ref[:, cols], preferred_element_type=f32
        ).astype(bf16)
        return carry

    lax.fori_loop(0, width // block, step, 0)


def unpack_kernel(capacity, width, ids_ref, rows_ref, x_ref, prob_ref):
    first, second = one_hots(ids_ref[...], capacity)
    hot = (first + second).astype(bf16)
    block = block_of(width)

    def step(i, carry):
        cols = pl.ds(pl.multiple_of(i * block, block), block)
        x_ref[:, cols] = lax.dot_general(
            hot, rows_ref[:, cols], (((0,), (0,)), ((), ())), preferred_element_type=f32
        ).astype(bf16)
        return carry

    lax.fori_loop(0, width // block, step, 0)
    q_col = rows_ref[:, width:].astype(f32)
    prob_ref[0:1, :] = jnp.sum(first * q_col, axis=0, keepdims=True).astype(bf16)
    prob_ref[1:2, :] = jnp.sum(second * q_col, axis=0, keepdims=True).astype(bf16)


def vmem_specs(count):
    return [pl.BlockSpec(memory_space=pltpu.VMEM) for _ in range(count)]


def pack_rows(ids, probs, x, y, capacity):
    width = x.shape[1]
    return pl.pallas_call(
        lambda *refs: pack_kernel(capacity, width, *refs),
        out_shape=jax.ShapeDtypeStruct((GROUPS * capacity, 2 * width + LANES), bf16),
        in_specs=vmem_specs(4),
        out_specs=vmem_specs(1)[0],
        compiler_params=pltpu.CompilerParams(vmem_limit_bytes=40 << 20),
        name="pack_rows",
    )(ids, probs, x, y)


def unpack_rows(ids, rows, width, capacity):
    tok = ids.shape[1]
    return pl.pallas_call(
        lambda *refs: unpack_kernel(capacity, width, *refs),
        out_shape=(
            jax.ShapeDtypeStruct((tok, width), bf16),
            jax.ShapeDtypeStruct((2, tok), bf16),
        ),
        in_specs=vmem_specs(2),
        out_specs=tuple(vmem_specs(2)),
        compiler_params=pltpu.CompilerParams(vmem_limit_bytes=40 << 20),
        name="unpack_rows",
    )(ids, rows)


def term_kernel(x_ref, gate_ref, up_ref, gate_out, up_out):
    for d_ref, out in ((gate_ref, gate_out), (up_ref, up_out)):
        out[...] = lax.dot_general(
            x_ref[...], d_ref[...], (((0,), (0,)), ((), ())), preferred_element_type=f32
        ).astype(bf16)


SMALL = pl.CostEstimate(flops=1, transcendentals=0, bytes_accessed=1)


def x_terms(x_rows, gate_grad, up_grad):
    count, width = x_rows.shape
    n = gate_grad.shape[1]
    block = block_of(width)
    out = jax.ShapeDtypeStruct((width, n), bf16)
    whole = pl.BlockSpec((count, n), lambda i: (0, 0))
    part = pl.BlockSpec((block, n), lambda i: (i, 0))
    return pl.pallas_call(
        term_kernel,
        out_shape=(out, out),
        grid=(width // block,),
        in_specs=[pl.BlockSpec((count, block), lambda i: (0, i)), whole, whole],
        out_specs=(part, part),
        cost_estimate=SMALL,
        compiler_params=pltpu.CompilerParams(vmem_limit_bytes=40 << 20),
        name="x_terms",
    )(x_rows, gate_grad, up_grad)


def row_kernel(gate_ref, up_ref, w_ref, out_ref):
    half = gate_ref.shape[1]
    total = lax.dot_general(
        gate_ref[...], w_ref[:, :half], (((1,), (1,)), ((), ())), preferred_element_type=f32
    )
    total += lax.dot_general(
        up_ref[...], w_ref[:, half:], (((1,), (1,)), ((), ())), preferred_element_type=f32
    )
    out_ref[...] = total.astype(bf16)


def input_rows(gate_grad, up_grad, w_gate_up):
    count, n = gate_grad.shape
    width = w_gate_up.shape[0]
    block = block_of(width)
    whole = pl.BlockSpec((count, n), lambda i: (0, 0))
    return pl.pallas_call(
        row_kernel,
        out_shape=jax.ShapeDtypeStruct((count, width), bf16),
        grid=(width // block,),
        in_specs=[whole, whole, pl.BlockSpec((block, 2 * n), lambda i: (i, 0))],
        out_specs=pl.BlockSpec((count, block), lambda i: (0, i)),
        cost_estimate=SMALL,
        compiler_params=pltpu.CompilerParams(vmem_limit_bytes=40 << 20),
        name="input_rows",
    )(gate_grad, up_grad, w_gate_up)


def put_kernel(count, rows_ref, *refs):
    pieces, out_ref, sems = refs[:count], refs[-2], refs[-1]
    copies = [
        pltpu.make_async_copy(
            piece,
            out_ref.at[pl.ds(pl.multiple_of(rows_ref[i], 16), piece.shape[0])],
            sems.at[i],
        )
        for i, piece in enumerate(pieces)
    ]
    for copy in copies:
        copy.start()
    for copy in copies:
        copy.wait()


def put(whole, height, placed):
    pieces = [piece for piece, _ in placed]
    count = len(pieces)
    starts = jnp.stack([row for _, row in placed]).astype(jnp.int32)
    old = [] if whole is None else [whole]
    out = jax.ShapeDtypeStruct((height, pieces[0].shape[1]), bf16)
    moved = sum(piece.size for piece in pieces) * 4
    return pl.pallas_call(
        lambda *refs: put_kernel(count, *refs),
        out_shape=out,
        in_specs=[pl.BlockSpec(memory_space=pltpu.SMEM)]
        + vmem_specs(count)
        + [pl.BlockSpec(memory_space=pl.ANY) for _ in old],
        out_specs=pl.BlockSpec(memory_space=pl.ANY),
        scratch_shapes=[pltpu.SemaphoreType.DMA((count,))],
        input_output_aliases={1 + count: 0} if old else {},
        cost_estimate=pl.CostEstimate(flops=0, transcendentals=0, bytes_accessed=moved),
        compiler_params=pltpu.CompilerParams(vmem_limit_bytes=40 << 20),
        name="put_rows",
    )(starts, *pieces, *old)


def neighbours(part):
    return lax.ppermute(part, "x", PLUS), lax.ppermute(part, "x", MINUS)


def far(left, right, half):
    return lax.ppermute(left[:half], "x", PLUS), lax.ppermute(right[half:], "x", MINUS)


def plus(*values):
    return sum(v.astype(f32) for v in values).astype(bf16)


def send(pair):
    to_right, to_left = pair
    return lax.ppermute(to_right, "x", PLUS), lax.ppermute(to_left, "x", MINUS)


class Scatter:
    def __init__(self, terms, x, yh):
        self.terms, self.x, self.yh = terms, x, yh
        self.size, self.n = terms.shape[0] // 8, terms.shape[1]

    def rows(self, k, side, count):
        start = self.size * (2 * ((self.x + k) % 4) + side)
        return lax.dynamic_slice(self.terms, (start, 0), (count * self.size, self.n))

    def first(self):
        to_right = jnp.concatenate((self.rows(2, 0, 1), self.rows(1, 1, 1)))
        to_left = jnp.concatenate((self.rows(2, 1, 1), self.rows(3, 0, 1)))
        return to_right, to_left

    def second(self, got):
        from_left, from_right = got
        self.low, self.top = from_left[self.size :], from_right[self.size :]
        to_right = plus(self.rows(1, 0, 1), from_left[: self.size])
        to_left = plus(self.rows(3, 1, 1), from_right[: self.size])
        return to_right, to_left

    def mine(self, side):
        top, low = self.got
        return plus(
            self.rows(0, side, 1),
            jnp.where(side == 0, top, self.low),
            jnp.where(side == 0, self.top, low),
        )

    def third(self):
        self.kept = self.mine(self.yh)
        return lax.ppermute(self.mine(1 - self.yh), "yh", SWAP)

    def last(self, sent):
        return plus(self.kept, sent)


def body(
    layer_input,
    output_grad,
    expert_ids,
    gate_probs,
    gate_weight,
    up_weight,
    down_weight,
    gate_moment,
    up_moment,
    down_moment,
    gate_second,
    up_second,
    down_second,
):
    x, yh, yl = lax.axis_index("x"), lax.axis_index("yh"), lax.axis_index("yl")
    z, c = lax.axis_index("z"), lax.axis_index("c")
    tok, picks = expert_ids.shape
    capacity = 3 * tok * picks // (2 * GROUPS)
    width = layer_input.shape[1]
    hidden_units = gate_weight.shape[2]
    quarter = hidden_units // 4
    half = hidden_units // 2
    rows = GROUPS * capacity
    depth = gate_weight.shape[1]

    gate_low, up_low = gate_weight[0].astype(bf16), up_weight[0].astype(bf16)

    def chunk(core):
        cuts = [
            w[:, (core + 2 * k) * quarter : (core + 2 * k + 1) * quarter]
            for w in (gate_low, up_low)
            for k in range(2)
        ]
        return jnp.concatenate(cuts, axis=1)

    chunks = (chunk(0), chunk(1))
    part_a = lax.ppermute(jnp.where(yl == 0, chunks[0], chunks[1]), ("yl", "c"), PAIR_A)
    part_b = lax.ppermute(jnp.where(yl == 0, chunks[1], chunks[0]), ("yl", "c"), PAIR_B)
    down_part = lax.ppermute(down_weight[0].astype(bf16), CYCLE_AXES, CYCLE)
    part_a, part_b, down_part = join((part_a, part_b, down_part))
    part = jnp.where(
        c == 0, jnp.concatenate((part_a, part_b)), jnp.concatenate((part_b, part_a))
    )

    part_other = lax.ppermute(part, "yh", SWAP)
    down_other = lax.ppermute(down_part, "yh", SWAP)
    near_own = join(neighbours(part))
    far_own = far(*near_own, depth)
    ids = expert_ids.T
    sent = pack_rows(ids, gate_probs.T.astype(f32), layer_input, output_grad, capacity)
    sent, part_other, down_other, far_own = join((sent, part_other, down_other, far_own))

    size_down = down_part.shape[0]
    both = jnp.where(
        yh == 0,
        jnp.concatenate((down_part, down_other)),
        jnp.concatenate((down_other, down_part)),
    )

    def gate_up_row(k, side):
        return 2 * depth * (2 * ((x + k) % 4) + side)

    def down_row(k):
        return 2 * size_down * ((x + k) % 4)

    def ring_rows(row, part, left, right):
        return [(part, row(0)), (left, row(3)), (right, row(1))]

    def far_rows_of(row, top, low):
        return [(top, row(2)), (low, row(2) + top.shape[0])]

    own_row = lambda k: gate_up_row(k, yh)
    other_row = lambda k: gate_up_row(k, 1 - yh)
    near_other = neighbours(part_other)
    own = lax.all_to_all(
        sent.reshape(GROUPS, capacity, -1), ("yl", "z"), 0, 0, tiled=True
    ).reshape(rows, -1)
    w_gate_up = put(
        None,
        width,
        ring_rows(own_row, part, *near_own) + far_rows_of(own_row, *far_own),
    )
    near_other, w_gate_up, both = join((near_other, w_gate_up, both))
    near_down = neighbours(both)
    far_other = far(*near_other, depth)
    w_gate_up = put(w_gate_up, width, ring_rows(other_row, part_other, *near_other))
    own, near_down, far_other, w_gate_up = join((own, near_down, far_other, w_gate_up))
    far_down = far(*near_down, size_down)
    w_gate_up = put(w_gate_up, width, far_rows_of(other_row, *far_other))
    w_down = put(None, half, ring_rows(down_row, both, *near_down))
    other = lax.ppermute(own, "c", SWAP)
    x_rows = jnp.concatenate((own[:, :width], other[:, :width]))
    y_rows = jnp.concatenate((own[:, width : 2 * width], other[:, width : 2 * width]))
    gates = jnp.concatenate((own[:, 2 * width :], other[:, 2 * width :]))[:, :1].astype(f32)

    pre = jnp.dot(x_rows, w_gate_up, preferred_element_type=f32)
    gate_pre, up_pre = pre[:, :half], pre[:, half:]
    sigmoid_gate = jax.nn.sigmoid(gate_pre)
    silu_gate = gate_pre * sigmoid_gate
    hidden_full = silu_gate * up_pre
    hidden = hidden_full.astype(bf16)
    hidden_scaled = (gates * hidden_full).astype(bf16)
    down_term = lax.dot_general(
        hidden_scaled, y_rows, (((0,), (0,)), ((), ())), preferred_element_type=f32
    ).astype(bf16)
    down_sum = Scatter(down_term, x, yh)
    down_send = down_sum.first()
    far_down, down_send = join((far_down, down_send))
    w_down = put(w_down, half, far_rows_of(down_row, *far_down))
    down_got = send(down_send)
    raw_grad = lax.dot_general(
        y_rows, w_down, (((1,), (1,)), ((), ())), preferred_element_type=f32
    )
    prob_rows = jnp.sum(hidden.astype(f32) * raw_grad, axis=1, keepdims=True)
    hidden_grad = gates * raw_grad
    dsilu = sigmoid_gate * (1.0 + gate_pre * (1.0 - sigmoid_gate))
    gate_grad = (hidden_grad * up_pre * dsilu).astype(bf16)
    up_grad = (hidden_grad * silu_gate).astype(bf16)

    gate_term, up_term = x_terms(x_rows, gate_grad, up_grad)
    gate_sum, up_sum = Scatter(gate_term, x, yh), Scatter(up_term, x, yh)

    far_part = input_rows(gate_grad[rows:], up_grad[rows:], w_gate_up)
    far_prob = jnp.broadcast_to(prob_rows[rows:], (rows, LANES))
    far_prob = lax.ppermute(far_prob, "c", SWAP)
    gate_send = gate_sum.first()
    down_got, gate_send, far_part, far_prob = join((down_got, gate_send, far_part, far_prob))
    down_send = down_sum.second(down_got)
    gate_grad, up_grad, down_send, gate_send = join(
        (gate_grad, up_grad, down_send, gate_send)
    )
    down_got, gate_got = send(down_send), send(gate_send)
    far_rows = lax.ppermute(far_part, "c", SWAP)
    near_rows = (
        input_rows(gate_grad[:rows], up_grad[:rows], w_gate_up).astype(f32)
        + far_rows.astype(f32)
    ).astype(bf16)
    near_prob = (prob_rows[:rows] + far_prob).astype(bf16)
    packed = jnp.concatenate((near_rows, near_prob), axis=1)
    gate_got, down_sum.got = join((gate_got, down_got))
    gate_send, up_send = join((gate_sum.second(gate_got), up_sum.first()))
    gate_got, up_got = send(gate_send), send(up_send)
    down_sent = down_sum.third()
    returned = lax.all_to_all(
        packed.reshape(GROUPS, capacity, -1), ("yl", "z"), 0, 0, tiled=True
    ).reshape(rows, -1)
    up_got, gate_sum.got, down_sent, returned = join((up_got, gate_got, down_sent, returned))

    def send_home(grad):
        return tuple(
            lax.ppermute(
                lax.dynamic_slice(grad, (depth * start, 0), (depth, half)),
                ("yl", "c"),
                back(pairs),
            )
            for start, pairs in ((c, PAIR_A), (1 - c, PAIR_B))
        )

    def natural(home):
        even = jnp.where(yl == 0, home[0], home[1])
        odd = jnp.where(yl == 0, home[1], home[0])
        return jnp.concatenate(
            [v[:, k * quarter : (k + 1) * quarter] for k in range(2) for v in (even, odd)],
            axis=1,
        )[None].astype(f32)

    down_home = down_sum.last(down_sent)
    up_send, gate_sum.got, down_home = join((up_sum.second(up_got), gate_sum.got, down_home))
    up_got = send(up_send)
    gate_sent = gate_sum.third()
    down_home = lax.ppermute(down_home, CYCLE_AXES, back(CYCLE))
    up_sum.got, gate_sent, down_home = join((up_got, gate_sent, down_home))
    up_mine, gate_sent = join((up_sum.mine(1 - yh), gate_sent))
    up_sent = lax.ppermute(up_mine, "yh", SWAP)
    up_sum.kept = up_sum.mine(yh)
    gate_home = send_home(gate_sum.last(gate_sent))
    new_down_weight, new_down_moment, new_down_second = adamw(
        down_weight, down_moment, down_second, down_home.astype(f32)[None]
    )
    up_sent, gate_home = join((up_sent, gate_home))
    up_home = send_home(up_sum.last(up_sent))
    input_grad, prob_grad = unpack_rows(ids, returned, width, capacity)
    new_gate_weight, new_gate_moment, new_gate_second = adamw(
        gate_weight, gate_moment, gate_second, natural(gate_home)
    )
    up_home, new_gate_weight = join((up_home, new_gate_weight))
    new_up_weight, new_up_moment, new_up_second = adamw(
        up_weight, up_moment, up_second, natural(up_home)
    )
    return (
        input_grad,
        prob_grad.T,
        new_gate_weight,
        new_up_weight,
        new_down_weight,
        new_gate_moment,
        new_up_moment,
        new_down_moment,
        new_gate_second,
        new_up_second,
        new_down_second,
    )


def solution(mesh):
    fine = Mesh(mesh.devices.reshape(4, 2, 2, 4, 2), ("x", "yh", "yl", "z", "c"))
    tokens = P(("x", "yh", "yl", "z", "c"), None)
    weights = P(("z", "c"), ("x", "yh", "yl"), None)
    return jax.shard_map(
        body,
        mesh=fine,
        in_specs=(tokens,) * 4 + (weights,) * 9,
        out_specs=(tokens,) * 2 + (weights,) * 9,
        check_vma=False,
    )
```

```python
import jax
import jax.numpy as jnp
from jax import lax
from jax.experimental import pallas as pl
from jax.experimental.pallas import tpu as pltpu
from jax.sharding import Mesh
from jax.sharding import PartitionSpec as P

beta_one = 0.9
beta_two = 0.95
learn_rate = 0.003
decay_rate = 0.1
epsilon = 1e-08
correct_one = 1.0 - 2.6561398887587e-05
correct_two = 1.0 - 0.005920529220333

LANES = 128
GROUPS = 8
f32 = jnp.float32
bf16 = jnp.bfloat16

PLUS = [(i, (i + 1) % 4) for i in range(4)]
MINUS = [(i, (i - 1) % 4) for i in range(4)]
SWAP = [(0, 1), (1, 0)]
PAIR_A = [(2 * yl + c, 2 * c + yl) for yl in range(2) for c in range(2)]
PAIR_B = [(2 * yl + c, 2 * c + 1 - yl) for yl in range(2) for c in range(2)]


def _cycle():
    pairs = []
    for x1 in range(2):
        for x0 in range(2):
            for yh in range(2):
                for yl in range(2):
                    for c in range(2):
                        src = (((x1 * 2 + x0) * 2 + yh) * 2 + yl) * 2 + c
                        dst = (((x1 * 2 + yh) * 2 + yl) * 2 + c) * 2 + x0
                        pairs.append((src, dst))
    return pairs


CYCLE = _cycle()
CYCLE_AXES = ("x", "yh", "yl", "c")


def back(pairs):
    return [(d, s) for s, d in pairs]


join = lax.optimization_barrier


def adamw(weight, moment, second, grad):
    moment_new = beta_one * moment + (1.0 - beta_one) * grad
    second_new = beta_two * second + (1.0 - beta_two) * grad * grad
    update = moment_new / correct_one / (jnp.sqrt(second_new / correct_two) + epsilon)
    return (weight - learn_rate * (update + decay_rate * weight), moment_new, second_new)


def one_hots(ids, capacity):
    tok = ids.shape[1]
    experts = lax.broadcasted_iota(jnp.int32, (GROUPS, tok), 0)
    named = [(experts == ids[k : k + 1, :]).astype(f32) for k in range(2)]
    earlier = (
        lax.broadcasted_iota(jnp.int32, (tok, tok), 0)
        < lax.broadcasted_iota(jnp.int32, (tok, tok), 1)
    ).astype(f32)
    count = jnp.dot(
        (named[0] + named[1]).astype(bf16), earlier.astype(bf16), preferred_element_type=f32
    )
    slot = lax.broadcasted_iota(jnp.int32, (GROUPS * capacity, tok), 0)
    hots = []
    for k in range(2):
        rank = jnp.sum(named[k] * count, axis=0, keepdims=True).astype(jnp.int32)
        expert = ids[k : k + 1, :]
        dest = ((expert & 1) * 4 + (expert >> 1)) * capacity + rank
        hots.append((slot == dest).astype(f32))
    return hots


def block_of(width):
    return 512 if width % 512 == 0 else width


def pack_kernel(capacity, width, ids_ref, probs_ref, x_ref, y_ref, out_ref):
    first, second = one_hots(ids_ref[...], capacity)
    hot = (first + second).astype(bf16)
    probs = probs_ref[...]
    gates = (first * probs[0:1, :] + second * probs[1:2, :]).astype(bf16)
    ones = jnp.ones((gates.shape[1], LANES), bf16)
    out_ref[:, 2 * width :] = jnp.dot(gates, ones, preferred_element_type=f32).astype(bf16)
    block = block_of(width)

    def step(i, carry):
        at = pl.multiple_of(i * block, block)
        cols = pl.ds(at, block)
        out_ref[:, cols] = jnp.dot(
            hot, x_ref[:, cols], preferred_element_type=f32
        ).astype(bf16)
        out_ref[:, pl.ds(pl.multiple_of(at + width, block), block)] = jnp.dot(
            hot, y_ref[:, cols], preferred_element_type=f32
        ).astype(bf16)
        return carry

    lax.fori_loop(0, width // block, step, 0)


def unpack_kernel(capacity, width, ids_ref, rows_ref, x_ref, prob_ref):
    first, second = one_hots(ids_ref[...], capacity)
    hot = (first + second).astype(bf16)
    block = block_of(width)

    def step(i, carry):
        cols = pl.ds(pl.multiple_of(i * block, block), block)
        x_ref[:, cols] = lax.dot_general(
            hot, rows_ref[:, cols], (((0,), (0,)), ((), ())), preferred_element_type=f32
        ).astype(bf16)
        return carry

    lax.fori_loop(0, width // block, step, 0)
    q_col = rows_ref[:, width:].astype(f32)
    prob_ref[0:1, :] = jnp.sum(first * q_col, axis=0, keepdims=True).astype(bf16)
    prob_ref[1:2, :] = jnp.sum(second * q_col, axis=0, keepdims=True).astype(bf16)


def vmem_specs(count):
    return [pl.BlockSpec(memory_space=pltpu.VMEM) for _ in range(count)]


def pack_rows(ids, probs, x, y, capacity):
    width = x.shape[1]
    return pl.pallas_call(
        lambda *refs: pack_kernel(capacity, width, *refs),
        out_shape=jax.ShapeDtypeStruct((GROUPS * capacity, 2 * width + LANES), bf16),
        in_specs=vmem_specs(4),
        out_specs=vmem_specs(1)[0],
        compiler_params=pltpu.CompilerParams(vmem_limit_bytes=40 << 20),
        name="pack_rows",
    )(ids, probs, x, y)


def unpack_rows(ids, rows, width, capacity):
    tok = ids.shape[1]
    return pl.pallas_call(
        lambda *refs: unpack_kernel(capacity, width, *refs),
        out_shape=(
            jax.ShapeDtypeStruct((tok, width), bf16),
            jax.ShapeDtypeStruct((2, tok), bf16),
        ),
        in_specs=vmem_specs(2),
        out_specs=tuple(vmem_specs(2)),
        compiler_params=pltpu.CompilerParams(vmem_limit_bytes=40 << 20),
        name="unpack_rows",
    )(ids, rows)


def term_kernel(x_ref, gate_ref, up_ref, gate_out, up_out):
    for d_ref, out in ((gate_ref, gate_out), (up_ref, up_out)):
        out[...] = lax.dot_general(
            x_ref[...], d_ref[...], (((0,), (0,)), ((), ())), preferred_element_type=f32
        ).astype(bf16)


SMALL = pl.CostEstimate(flops=1, transcendentals=0, bytes_accessed=1)


def x_terms(x_rows, gate_grad, up_grad):
    count, width = x_rows.shape
    n = gate_grad.shape[1]
    block = block_of(width)
    out = jax.ShapeDtypeStruct((width, n), bf16)
    whole = pl.BlockSpec((count, n), lambda i: (0, 0))
    part = pl.BlockSpec((block, n), lambda i: (i, 0))
    return pl.pallas_call(
        term_kernel,
        out_shape=(out, out),
        grid=(width // block,),
        in_specs=[pl.BlockSpec((count, block), lambda i: (0, i)), whole, whole],
        out_specs=(part, part),
        cost_estimate=SMALL,
        compiler_params=pltpu.CompilerParams(vmem_limit_bytes=40 << 20),
        name="x_terms",
    )(x_rows, gate_grad, up_grad)


def row_kernel(gate_ref, up_ref, w_ref, out_ref):
    half = gate_ref.shape[1]
    total = lax.dot_general(
        gate_ref[...], w_ref[:, :half], (((1,), (1,)), ((), ())), preferred_element_type=f32
    )
    total += lax.dot_general(
        up_ref[...], w_ref[:, half:], (((1,), (1,)), ((), ())), preferred_element_type=f32
    )
    out_ref[...] = total.astype(bf16)


def input_rows(gate_grad, up_grad, w_gate_up):
    count, n = gate_grad.shape
    width = w_gate_up.shape[0]
    block = block_of(width)
    whole = pl.BlockSpec((count, n), lambda i: (0, 0))
    return pl.pallas_call(
        row_kernel,
        out_shape=jax.ShapeDtypeStruct((count, width), bf16),
        grid=(width // block,),
        in_specs=[whole, whole, pl.BlockSpec((block, 2 * n), lambda i: (i, 0))],
        out_specs=pl.BlockSpec((count, block), lambda i: (0, i)),
        cost_estimate=SMALL,
        compiler_params=pltpu.CompilerParams(vmem_limit_bytes=40 << 20),
        name="input_rows",
    )(gate_grad, up_grad, w_gate_up)


def put_kernel(count, rows_ref, *refs):
    pieces, out_ref, sems = refs[:count], refs[-2], refs[-1]
    copies = [
        pltpu.make_async_copy(
            piece,
            out_ref.at[pl.ds(pl.multiple_of(rows_ref[i], 16), piece.shape[0])],
            sems.at[i],
        )
        for i, piece in enumerate(pieces)
    ]
    for copy in copies:
        copy.start()
    for copy in copies:
        copy.wait()


def put(whole, height, placed):
    pieces = [piece for piece, _ in placed]
    count = len(pieces)
    starts = jnp.stack([row for _, row in placed]).astype(jnp.int32)
    old = [] if whole is None else [whole]
    out = jax.ShapeDtypeStruct((height, pieces[0].shape[1]), bf16)
    moved = sum(piece.size for piece in pieces) * 4
    return pl.pallas_call(
        lambda *refs: put_kernel(count, *refs),
        out_shape=out,
        in_specs=[pl.BlockSpec(memory_space=pltpu.SMEM)]
        + vmem_specs(count)
        + [pl.BlockSpec(memory_space=pl.ANY) for _ in old],
        out_specs=pl.BlockSpec(memory_space=pl.ANY),
        scratch_shapes=[pltpu.SemaphoreType.DMA((count,))],
        input_output_aliases={1 + count: 0} if old else {},
        cost_estimate=pl.CostEstimate(flops=0, transcendentals=0, bytes_accessed=moved),
        compiler_params=pltpu.CompilerParams(vmem_limit_bytes=40 << 20),
        name="put_rows",
    )(starts, *pieces, *old)


def neighbours(part):
    return lax.ppermute(part, "x", PLUS), lax.ppermute(part, "x", MINUS)


def far(left, right, half):
    return lax.ppermute(left[:half], "x", PLUS), lax.ppermute(right[half:], "x", MINUS)


def plus(*values):
    return sum(v.astype(f32) for v in values).astype(bf16)


def send(pair):
    to_right, to_left = pair
    return lax.ppermute(to_right, "x", PLUS), lax.ppermute(to_left, "x", MINUS)


class Scatter:
    def __init__(self, terms, x, yh):
        self.terms, self.x, self.yh = terms, x, yh
        self.size, self.n = terms.shape[0] // 8, terms.shape[1]

    def rows(self, k, side, count):
        start = self.size * (2 * ((self.x + k) % 4) + side)
        return lax.dynamic_slice(self.terms, (start, 0), (count * self.size, self.n))

    def first(self):
        to_right = jnp.concatenate((self.rows(2, 0, 1), self.rows(1, 1, 1)))
        to_left = jnp.concatenate((self.rows(2, 1, 1), self.rows(3, 0, 1)))
        return to_right, to_left

    def second(self, got):
        from_left, from_right = got
        self.low, self.top = from_left[self.size :], from_right[self.size :]
        to_right = plus(self.rows(1, 0, 1), from_left[: self.size])
        to_left = plus(self.rows(3, 1, 1), from_right[: self.size])
        return to_right, to_left

    def mine(self, side):
        top, low = self.got
        return plus(
            self.rows(0, side, 1),
            jnp.where(side == 0, top, self.low),
            jnp.where(side == 0, self.top, low),
        )

    def third(self):
        self.kept = self.mine(self.yh)
        return lax.ppermute(self.mine(1 - self.yh), "yh", SWAP)

    def last(self, sent):
        return plus(self.kept, sent)


def body(
    layer_input,
    output_grad,
    expert_ids,
    gate_probs,
    gate_weight,
    up_weight,
    down_weight,
    gate_moment,
    up_moment,
    down_moment,
    gate_second,
    up_second,
    down_second,
):
    x, yh, yl = lax.axis_index("x"), lax.axis_index("yh"), lax.axis_index("yl")
    z, c = lax.axis_index("z"), lax.axis_index("c")
    tok, picks = expert_ids.shape
    capacity = 3 * tok * picks // (2 * GROUPS)
    width = layer_input.shape[1]
    hidden_units = gate_weight.shape[2]
    quarter = hidden_units // 4
    half = hidden_units // 2
    rows = GROUPS * capacity
    depth = gate_weight.shape[1]

    gate_low, up_low = gate_weight[0].astype(bf16), up_weight[0].astype(bf16)

    def chunk(core):
        cuts = [
            w[:, (core + 2 * k) * quarter : (core + 2 * k + 1) * quarter]
            for w in (gate_low, up_low)
            for k in range(2)
        ]
        return jnp.concatenate(cuts, axis=1)

    chunks = (chunk(0), chunk(1))
    part_a = lax.ppermute(jnp.where(yl == 0, chunks[0], chunks[1]), ("yl", "c"), PAIR_A)
    part_b = lax.ppermute(jnp.where(yl == 0, chunks[1], chunks[0]), ("yl", "c"), PAIR_B)
    down_part = lax.ppermute(down_weight[0].astype(bf16), CYCLE_AXES, CYCLE)
    part_a, part_b, down_part = join((part_a, part_b, down_part))
    part = jnp.where(
        c == 0, jnp.concatenate((part_a, part_b)), jnp.concatenate((part_b, part_a))
    )

    part_other = lax.ppermute(part, "yh", SWAP)
    down_other = lax.ppermute(down_part, "yh", SWAP)
    near_own = join(neighbours(part))
    far_own = far(*near_own, depth)
    ids = expert_ids.T
    sent = pack_rows(ids, gate_probs.T.astype(f32), layer_input, output_grad, capacity)
    sent, part_other, down_other, far_own = join((sent, part_other, down_other, far_own))

    size_down = down_part.shape[0]
    both = jnp.where(
        yh == 0,
        jnp.concatenate((down_part, down_other)),
        jnp.concatenate((down_other, down_part)),
    )

    def gate_up_row(k, side):
        return 2 * depth * (2 * ((x + k) % 4) + side)

    def down_row(k):
        return 2 * size_down * ((x + k) % 4)

    def ring_rows(row, part, left, right):
        return [(part, row(0)), (left, row(3)), (right, row(1))]

    def far_rows_of(row, top, low):
        return [(top, row(2)), (low, row(2) + top.shape[0])]

    own_row = lambda k: gate_up_row(k, yh)
    other_row = lambda k: gate_up_row(k, 1 - yh)
    near_other = neighbours(part_other)
    own = lax.all_to_all(
        sent.reshape(GROUPS, capacity, -1), ("yl", "z"), 0, 0, tiled=True
    ).reshape(rows, -1)
    w_gate_up = put(
        None,
        width,
        ring_rows(own_row, part, *near_own) + far_rows_of(own_row, *far_own),
    )
    near_other, w_gate_up, both = join((near_other, w_gate_up, both))
    near_down = neighbours(both)
    far_other = far(*near_other, depth)
    w_gate_up = put(w_gate_up, width, ring_rows(other_row, part_other, *near_other))
    own, near_down, far_other, w_gate_up = join((own, near_down, far_other, w_gate_up))
    far_down = far(*near_down, size_down)
    w_gate_up = put(w_gate_up, width, far_rows_of(other_row, *far_other))
    w_down = put(None, half, ring_rows(down_row, both, *near_down))
    other = lax.ppermute(own, "c", SWAP)
    x_rows = jnp.concatenate((own[:, :width], other[:, :width]))
    y_rows = jnp.concatenate((own[:, width : 2 * width], other[:, width : 2 * width]))
    gates = jnp.concatenate((own[:, 2 * width :], other[:, 2 * width :]))[:, :1].astype(f32)

    pre = jnp.dot(x_rows, w_gate_up, preferred_element_type=f32)
    gate_pre, up_pre = pre[:, :half], pre[:, half:]
    sigmoid_gate = jax.nn.sigmoid(gate_pre)
    silu_gate = gate_pre * sigmoid_gate
    hidden_full = silu_gate * up_pre
    hidden = hidden_full.astype(bf16)
    hidden_scaled = (gates * hidden_full).astype(bf16)
    down_term = lax.dot_general(
        hidden_scaled, y_rows, (((0,), (0,)), ((), ())), preferred_element_type=f32
    ).astype(bf16)
    down_sum = Scatter(down_term, x, yh)
    down_send = down_sum.first()
    far_down, down_send = join((far_down, down_send))
    w_down = put(w_down, half, far_rows_of(down_row, *far_down))
    down_got = send(down_send)
    raw_grad = lax.dot_general(
        y_rows, w_down, (((1,), (1,)), ((), ())), preferred_element_type=f32
    )
    prob_rows = jnp.sum(hidden.astype(f32) * raw_grad, axis=1, keepdims=True)
    hidden_grad = gates * raw_grad
    dsilu = sigmoid_gate * (1.0 + gate_pre * (1.0 - sigmoid_gate))
    gate_grad = (hidden_grad * up_pre * dsilu).astype(bf16)
    up_grad = (hidden_grad * silu_gate).astype(bf16)

    gate_term, up_term = x_terms(x_rows, gate_grad, up_grad)
    gate_sum, up_sum = Scatter(gate_term, x, yh), Scatter(up_term, x, yh)

    far_part = input_rows(gate_grad[rows:], up_grad[rows:], w_gate_up)
    far_prob = jnp.broadcast_to(prob_rows[rows:], (rows, LANES))
    far_prob = lax.ppermute(far_prob, "c", SWAP)
    gate_send = gate_sum.first()
    down_got, gate_send, far_part, far_prob = join((down_got, gate_send, far_part, far_prob))
    down_send = down_sum.second(down_got)
    gate_grad, up_grad, down_send, gate_send = join(
        (gate_grad, up_grad, down_send, gate_send)
    )
    down_got, gate_got = send(down_send), send(gate_send)
    far_rows = lax.ppermute(far_part, "c", SWAP)
    near_rows = (
        input_rows(gate_grad[:rows], up_grad[:rows], w_gate_up).astype(f32)
        + far_rows.astype(f32)
    ).astype(bf16)
    near_prob = (prob_rows[:rows] + far_prob).astype(bf16)
    packed = jnp.concatenate((near_rows, near_prob), axis=1)
    gate_got, down_sum.got = join((gate_got, down_got))
    gate_send, up_send = join((gate_sum.second(gate_got), up_sum.first()))
    gate_got, up_got = send(gate_send), send(up_send)
    down_sent = down_sum.third()
    returned = lax.all_to_all(
        packed.reshape(GROUPS, capacity, -1), ("yl", "z"), 0, 0, tiled=True
    ).reshape(rows, -1)
    up_got, gate_sum.got, down_sent, returned = join((up_got, gate_got, down_sent, returned))

    def send_home(grad):
        return tuple(
            lax.ppermute(
                lax.dynamic_slice(grad, (depth * start, 0), (depth, half)),
                ("yl", "c"),
                back(pairs),
            )
            for start, pairs in ((c, PAIR_A), (1 - c, PAIR_B))
        )

    def natural(home):
        even = jnp.where(yl == 0, home[0], home[1])
        odd = jnp.where(yl == 0, home[1], home[0])
        return jnp.concatenate(
            [v[:, k * quarter : (k + 1) * quarter] for k in range(2) for v in (even, odd)],
            axis=1,
        )[None].astype(f32)

    down_home = down_sum.last(down_sent)
    up_send, gate_sum.got, down_home = join((up_sum.second(up_got), gate_sum.got, down_home))
    up_got = send(up_send)
    gate_sent = gate_sum.third()
    down_home = lax.ppermute(down_home, CYCLE_AXES, back(CYCLE))
    up_sum.got, gate_sent, down_home = join((up_got, gate_sent, down_home))
    up_mine, gate_sent = join((up_sum.mine(1 - yh), gate_sent))
    up_sent = lax.ppermute(up_mine, "yh", SWAP)
    up_sum.kept, gate_sent = join((up_sum.mine(yh), gate_sent))
    new_down_weight, new_down_moment, new_down_second = adamw(
        down_weight, down_moment, down_second, down_home.astype(f32)[None]
    )
    gate_last, new_down_weight = join((gate_sum.last(gate_sent), new_down_weight))
    gate_home = send_home(gate_last)
    up_last = up_sum.last(up_sent)
    up_last, gate_home = join((up_last, gate_home))
    up_home = send_home(up_last)
    input_grad, prob_grad = unpack_rows(ids, returned, width, capacity)
    new_gate_weight, new_gate_moment, new_gate_second = adamw(
        gate_weight, gate_moment, gate_second, natural(gate_home)
    )
    up_home, new_gate_weight = join((up_home, new_gate_weight))
    new_up_weight, new_up_moment, new_up_second = adamw(
        up_weight, up_moment, up_second, natural(up_home)
    )
    return (
        input_grad,
        prob_grad.T,
        new_gate_weight,
        new_up_weight,
        new_down_weight,
        new_gate_moment,
        new_up_moment,
        new_down_moment,
        new_gate_second,
        new_up_second,
        new_down_second,
    )


def solution(mesh):
    fine = Mesh(mesh.devices.reshape(4, 2, 2, 4, 2), ("x", "yh", "yl", "z", "c"))
    tokens = P(("x", "yh", "yl", "z", "c"), None)
    weights = P(("z", "c"), ("x", "yh", "yl"), None)
    return jax.shard_map(
        body,
        mesh=fine,
        in_specs=(tokens,) * 4 + (weights,) * 9,
        out_specs=(tokens,) * 2 + (weights,) * 9,
        check_vma=False,
    )
```
